32 devices in a mesh: ctx: 4 (over y, core), ep: 8 (over z, x).
Axes of the slice: x: 2, y: 2, z: 4, core: 2. Of those that a mesh axis runs over, the one named last changes fastest.
Arguments:
- resid: bfloat16 [4096, 2048], P(('ctx', 'ep')), may hold values from -12 to 12
- mixed_qkv: bfloat16 [4096, 4096], P(('ctx', 'ep')), may hold values from -6 to 6
- out_gate: bfloat16 [4096, 2048], P(('ctx', 'ep')), may hold values from -6 to 6
- beta: float32 [16, 4096], P(None, ('ctx', 'ep')), may hold values from 0.001 to 0.95
- log_decay: float32 [16, 4096], P(None, ('ctx', 'ep')), may hold values from -1 to 0
- conv_weight: float32 [4, 4096], replicated, may hold values from -3 to 3
- head_gain: float32 [128], replicated, may hold values from 0.25 to 1.75
- moe_gain: float32 [2048], replicated, may hold values from 0.25 to 1.75
- routes: int32 [4096, 3], P(('ctx', 'ep')), may hold values from 0 to 7, all different within a row; in each aligned block of 128 rows (0 to 127, 128 to 255, ...) at most 60 rows name the same one
- route_gates: float32 [4096, 3], P(('ctx', 'ep')), may hold values from 0.1 to 1
- w_in: bfloat16 [8, 2048, 1024], P('ep', 'ctx'), may hold values from -0.125 to 0.125
- w_out: bfloat16 [8, 512, 2048], P('ep', None, 'ctx'), may hold values from -0.25 to 0.25
Outputs:
- mixer_out: bfloat16 [4096, 2048], P(('ctx', 'ep'))
- layer_out: bfloat16 [4096, 2048], P(('ctx', 'ep'))
The draws below stay inside these ranges and needn't reach their ends.
Inputs may be any that keep to these rules, and one draw needn't show every extreme that they name: `routes`: in the rows of one device no expert is named more than 60 times, a bound that some block reaches.
All inputs are finite; a program needn't handle non-finite values.
Results may differ from the reference program's by a relative error of at most 0.0037.
Values may be sent and summed in bfloat16 or wider, within the bound.
No kernel may reach another device: no remote copies, remote signals or barrier semaphores. Data moves between devices by JAX's collectives and lax.ppermute only.
A program may use at most 320 MiB of HBM per device.

```python
import math
import jax
import jax.numpy as jnp
import numpy as np
from jax import lax

HK = 8
VALUE_HEAD_SET = 16
DK = 128
DV = 128
D = 2048
MOE_H = 512
CONV = 4
TOPK = 3
TOK_DEV = 128
QKV = 4096
EXPERTS = 8
CAP = 60
TOKEN_COUNT = 4096
N_CTX = 4
N_EP = 8


def draw_beta(key, part):
    key_heads, key_weak, key_strong = jax.random.split(key, 3)
    order = jax.random.permutation(key_heads, VALUE_HEAD_SET)
    weak_mask = (order < VALUE_HEAD_SET // 2)[:, None]
    weak_u = jax.random.uniform(key_weak, (VALUE_HEAD_SET, TOKEN_COUNT))
    strong_u = jax.random.uniform(key_strong, (VALUE_HEAD_SET, TOKEN_COUNT))
    weak_vals = 0.001 + 0.009 * weak_u * weak_u
    strong_vals = 0.05 + 0.9 * strong_u
    return jnp.where(weak_mask, weak_vals, strong_vals).astype(jnp.float32)


def draw_log_decay(key, part):
    key_fast, key_block, key_jitter, key_position, key_magnitude = jax.random.split(key, 5)
    fast_share = 0.5
    fast_mask = jax.random.bernoulli(key_fast, fast_share, (VALUE_HEAD_SET, 1, 1))
    block_count = TOKEN_COUNT // TOK_DEV
    block_factor = jnp.exp(jax.random.uniform(key_block, (VALUE_HEAD_SET, block_count, 1), minval=-0.7, maxval=0.7))
    jitter = jnp.exp(jax.random.uniform(key_jitter, (VALUE_HEAD_SET, block_count, TOK_DEV), minval=-0.7, maxval=0.7))
    base_rate = jnp.where(fast_mask, 1.0 / 40.0, 0.4 / TOKEN_COUNT)
    logarithmic_rates = -(base_rate * block_factor * jitter).reshape(VALUE_HEAD_SET, TOKEN_COUNT)
    spike_positions = jax.random.randint(key_position, (VALUE_HEAD_SET, 2), 0, TOKEN_COUNT)
    spike_magnitude = jnp.log(jax.random.uniform(key_magnitude, (VALUE_HEAD_SET, 2), minval=0.5, maxval=0.8))
    match_mask = jnp.arange(TOKEN_COUNT)[None, None, :] == spike_positions[:, :, None]
    logarithmic_rates = logarithmic_rates + jnp.sum(jnp.where(match_mask, spike_magnitude[:, :, None], 0.0), axis=1)
    return logarithmic_rates.astype(jnp.float32)


def draw_resid(key, part):
    key_base, key_cols = jax.random.split(key, 2)
    col_scale = jnp.exp(jax.random.uniform(key_cols, (1, D), minval=-1.2, maxval=1.1))
    base_draw = jax.random.normal(key_base, (TOKEN_COUNT, D)) * col_scale
    return jnp.clip(base_draw, -12.0, 12.0).astype(jnp.bfloat16)


def block_scale(stream_key, extent, cuts, low, top_value):
    level, own = 1.0, jax.random.fold_in(stream_key, 6)
    for position, parts in cuts:
        heights = jnp.exp(jax.random.uniform(jax.random.fold_in(own, position), (parts,), jnp.float32, low / len(cuts), top_value / len(cuts)))
        level = level * jnp.repeat(heights, extent[position] // parts).reshape([-1 if axis == position else 1 for axis in range(len(extent))])
    return level


def assign_block(key, own, number, rows, number_of, top, reach, lean):
    sequence = jax.random.permutation(key, number_of)
    crowded, common = shares(number_of, rows * top, reach, lean, True), shares(number_of, rows * top, reach, lean, False)
    places = jnp.arange(number_of)

    def named(lengths, offset_by):
        used = int((lengths > 0).sum())
        fixed = max(1, used // 4)
        passed = fixed + (places - fixed + offset_by * (used - fixed)) % max(1, number_of - fixed)
        return jnp.zeros((number_of,), jnp.int32).at[sequence[jnp.where(places < fixed, places, passed)]].set(jnp.asarray(lengths, jnp.int32))

    lengths = jnp.where(number % 4 == 0, named(crowded, number // 4), named(common, number - number // 4 - 1))
    mixed = jax.random.permutation(jax.random.fold_in(own, 3), number_of)
    donor, sink = mixed[0:number_of // 2 * 2:2], mixed[1:number_of // 2 * 2:2]
    margin = jnp.minimum(lengths[donor] - 1, reach - lengths[sink]) // 2
    margin = jnp.where((donor == sequence[0]) | (sink == sequence[0]) | (lengths[sink] == 0), 0, jnp.maximum(margin, 0))
    passed = jax.random.randint(jax.random.fold_in(own, 4), (number_of // 2,), 0, 1 << 20) % (margin + 1)
    lengths = lengths.at[donor].add(-passed).at[sink].add(passed)
    items = jnp.searchsorted(jnp.cumsum(lengths), jnp.arange(rows * top), side="right").astype(jnp.int32)
    grid = items.reshape(top, rows).T
    grid = grid[jax.random.permutation(jax.random.fold_in(own, 1), rows)]
    offset_by = jax.random.randint(jax.random.fold_in(own, 2), (rows, 1), 0, top)
    return jnp.take_along_axis(grid, (jnp.arange(top)[None, :] + offset_by) % top, axis=1)


def shares(count, total, reach, slope, full):
    portions = [(1 << 20) // math.isqrt(grade ** slope) + 1 for grade in range(1, count + 1)]
    largest = reach if full else min(reach, max(-(-total // count), total * portions[0] // sum(portions)))
    least = 1 if total - largest >= count - 1 else 0
    holding, surplus = [largest] + [least] * (count - 1), total - largest - least * (count - 1)
    while surplus > 0:
        candidates = [i for i in range(1, count) if holding[i] < largest] or [i for i in range(1, count) if holding[i] < reach]
        mass, budget = sum([portions[i] for i in candidates]), surplus
        for i in candidates:
            more = min(reach - holding[i], max(1, budget * portions[i] // mass), surplus)
            holding[i] = holding[i] + more
            surplus = surplus - more
    return np.array(holding)


def centred(rng, shape, deviation, bound, cuts=(), held_as=jnp.bfloat16):
    level = block_scale(rng, shape, cuts, -0.22, 0.18) if cuts else 1.0
    drawn = jax.random.normal(rng, shape, jnp.float32) * deviation * level
    return jnp.minimum(jnp.maximum(drawn, -bound), bound).astype(held_as)


def setup_inputs(seed: int = 0) -> dict:
    splits = jax.random.split(jax.random.key(seed), 13)
    resid = draw_resid(jax.random.fold_in(splits[12], 71), 0)
    mixed_qkv = centred(splits[1], (TOKEN_COUNT, QKV), 1.0, 6.0, ((0, 32),))
    out_gate = centred(splits[2], (TOKEN_COUNT, D), 1.0, 6.0, ((0, 32),))
    beta = draw_beta(jax.random.fold_in(splits[12], 71), 0)
    log_decay = draw_log_decay(jax.random.fold_in(splits[12], 71), 0)
    conv_weight = centred(splits[5], (CONV, QKV), CONV ** -0.5, 3.0, (), jnp.float32)
    head_gain = jnp.clip(1.0 + 0.15 * jax.random.normal(splits[6], (DV,), jnp.float32), 0.25, 1.75)
    moe_gain = jnp.clip(1.0 + 0.15 * jax.random.normal(splits[7], (D,), jnp.float32), 0.25, 1.75)
    routes_keys = jax.random.split(jax.random.fold_in(splits[8], 1), TOKEN_COUNT // TOK_DEV)
    routes_turns = jax.random.permutation(jax.random.fold_in(splits[8], 3), TOKEN_COUNT // TOK_DEV)
    routes = jax.vmap(lambda own, number: assign_block(jax.random.fold_in(splits[8], 2), own, number, TOK_DEV, EXPERTS, TOPK, CAP, 2))(routes_keys, routes_turns).reshape((TOKEN_COUNT, TOPK))
    route_gates = jnp.clip(jnp.exp(math.log(1.0) - 2.3025851 * jax.random.uniform(splits[9], (TOKEN_COUNT, TOPK), jnp.float32) ** block_scale(splits[9], (TOKEN_COUNT, TOPK), ((0, 32),), -0.2, 0.2)), 0.1, 1.0)
    w_in = centred(splits[10], (EXPERTS, D, 2 * MOE_H), D ** -0.5, 0.125, ((0, 8), (1, 4)))
    w_out = centred(splits[11], (EXPERTS, MOE_H, D), MOE_H ** -0.5, 0.25, ((0, 8), (2, 4)))
    return dict(resid=resid, mixed_qkv=mixed_qkv, out_gate=out_gate, beta=beta, log_decay=log_decay, conv_weight=conv_weight, head_gain=head_gain, moe_gain=moe_gain, routes=routes, route_gates=route_gates, w_in=w_in, w_out=w_out)


precise = lax.Precision.HIGHEST

def short_conv(padded, conv_weight, row_count):
    qkv_data = padded.astype(jnp.float32)
    conv_sum = jnp.zeros((row_count, qkv_data.shape[1]), jnp.float32)
    for offset in range(conv_weight.shape[0]):
        conv_sum = conv_sum + qkv_data[offset:offset + row_count] * conv_weight[offset]
    return jax.nn.silu(conv_sum)

def local_terms(conv_out, beta, log_decay):
    row_count = conv_out.shape[0]
    head_group = VALUE_HEAD_SET // HK
    queries = conv_out[:, :HK * DK].reshape(row_count, HK, DK)
    keys_hat = conv_out[:, HK * DK:2 * HK * DK].reshape(row_count, HK, DK)
    values = conv_out[:, 2 * HK * DK:].reshape(row_count, VALUE_HEAD_SET, DV)
    queries = queries * lax.rsqrt(lax.optimization_barrier(jnp.sum(queries * queries, axis=-1, keepdims=True)) + 1e-06) * DK ** (-0.5)
    keys_hat = keys_hat * lax.rsqrt(lax.optimization_barrier(jnp.sum(keys_hat * keys_hat, axis=-1, keepdims=True)) + 1e-06)
    queries = jnp.repeat(queries, head_group, axis=1).transpose(1, 0, 2)
    keys_hat = jnp.repeat(keys_hat, head_group, axis=1).transpose(1, 0, 2)
    values = values.transpose(1, 0, 2)
    cumulative = jnp.cumsum(log_decay, axis=1)
    positions = jnp.arange(row_count)
    strict_mask = (positions[:, None] > positions[None, :])[None]
    causal_mask = (positions[:, None] >= positions[None, :])[None]
    log_gap = cumulative[:, :, None] - cumulative[:, None, :]
    fading = jnp.where(causal_mask, jnp.exp(jnp.where(causal_mask, log_gap, 0.0)), 0.0)
    key_key = jnp.einsum('htd,hsd->hts', keys_hat, keys_hat, precision=precise)
    mixing = jnp.where(strict_mask, beta[:, :, None] * fading * key_key, 0.0)
    identity_t = jnp.eye(row_count, dtype=jnp.float32)
    weights_solved = lax.linalg.triangular_solve(identity_t[None] + mixing, identity_t[None] * beta[:, :, None], left_side=True, lower=True)
    block_fade = jnp.exp(cumulative)
    tail_fade = jnp.exp(cumulative[:, -1:] - cumulative)
    fresh_vals = jnp.einsum('hts,hsv->htv', weights_solved, values, precision=precise)
    carried = jnp.einsum('hts,hsk->htk', weights_solved, block_fade[:, :, None] * keys_hat, precision=precise)
    faded_keys = tail_fade[:, :, None] * keys_hat
    transition = block_fade[:, -1][:, None, None] * jnp.eye(DK, dtype=jnp.float32)[None] - jnp.einsum('htj,htk->hjk', carried, faded_keys, precision=precise)
    state_add = jnp.einsum('htv,htk->hvk', fresh_vals, faded_keys, precision=precise)
    scores = fading * jnp.einsum('htd,hsd->hts', queries, keys_hat, precision=precise)
    return (queries, block_fade, scores, fresh_vals, carried, transition, state_add)

def head_outputs(queries, block_fade, scores, fresh_vals, carried, start_state):
    new_vals = fresh_vals - jnp.einsum('htk,hvk->htv', carried, start_state, precision=precise)
    from_state = jnp.einsum('htk,hvk->htv', queries, start_state, precision=precise)
    return block_fade[:, :, None] * from_state + jnp.einsum('hts,hsv->htv', scores, new_vals, precision=precise)

def gated_norm(head_out, out_gate, head_gain):
    row_count = head_out.shape[1]
    per_token = head_out.transpose(1, 0, 2)
    scaled = per_token * lax.rsqrt(lax.optimization_barrier(jnp.mean(per_token * per_token, axis=-1, keepdims=True)) + 1e-06) * head_gain
    gate_vals = out_gate.astype(jnp.float32).reshape(row_count, VALUE_HEAD_SET, DV)
    return (scaled * jax.nn.silu(gate_vals)).reshape(row_count, VALUE_HEAD_SET * DV).astype(jnp.bfloat16)

def reference(resid, mixed_qkv, out_gate, beta, log_decay, conv_weight, head_gain, moe_gain, routes, route_gates, w_in, w_out):
    block_count = TOKEN_COUNT // TOK_DEV
    qkv_blocks = mixed_qkv.reshape(block_count, TOK_DEV, QKV)
    gate_blocks = out_gate.reshape(block_count, TOK_DEV, D)
    beta_blocks = beta.reshape(VALUE_HEAD_SET, block_count, TOK_DEV).transpose(1, 0, 2)
    decay_blocks = log_decay.reshape(VALUE_HEAD_SET, block_count, TOK_DEV).transpose(1, 0, 2)

    def block_step(state_pair, inputs):
        state_now, rim_rows = state_pair
        qkv_block, gate_block, beta_block, decay_block = inputs
        conv_out = short_conv(jnp.concatenate([rim_rows, qkv_block], axis=0), conv_weight, TOK_DEV)
        queries, block_fade, scores, fresh_vals, carried, transition, state_add = local_terms(conv_out, beta_block, decay_block)
        head_out = head_outputs(queries, block_fade, scores, fresh_vals, carried, state_now)
        normed = gated_norm(head_out, gate_block, head_gain)
        state_next = jnp.einsum('hvj,hjk->hvk', state_now, transition, precision=precise) + state_add
        return ((state_next, qkv_block[TOK_DEV - CONV + 1:]), normed)
    start_pair = (jnp.zeros((VALUE_HEAD_SET, DV, DK), jnp.float32), jnp.zeros((CONV - 1, QKV), jnp.bfloat16))
    _, normed_blocks = lax.scan(block_step, start_pair, (qkv_blocks, gate_blocks, beta_blocks, decay_blocks))
    mixer_out = normed_blocks.reshape(TOKEN_COUNT, D)
    residual_mid = resid.astype(jnp.float32) + mixer_out.astype(jnp.float32)
    moe_input = (residual_mid * lax.rsqrt(lax.optimization_barrier(jnp.mean(residual_mid * residual_mid, axis=-1, keepdims=True)) + 1e-06) * moe_gain).astype(jnp.bfloat16)
    flat_routes = routes.reshape(-1)
    flat_gates = route_gates.reshape(-1)
    most_rows = N_CTX * N_EP * CAP

    def add_expert(expert, combined):
        chosen = flat_routes == expert
        picked = jnp.nonzero(chosen, size=most_rows, fill_value=0)[0]
        live_count = jnp.sum(chosen.astype(jnp.int32))
        live_mask = jnp.arange(most_rows) < live_count
        token_ids = picked // TOPK
        gathered = moe_input[token_ids]
        weight_in = lax.dynamic_index_in_dim(w_in, expert, 0, keepdims=False)
        weight_out = lax.dynamic_index_in_dim(w_out, expert, 0, keepdims=False)
        projected = jnp.dot(gathered.astype(jnp.float32), weight_in.astype(jnp.float32), preferred_element_type=jnp.float32)
        activated = (jax.nn.silu(projected[:, :MOE_H]) * projected[:, MOE_H:]).astype(jnp.bfloat16)
        expert_rows = jnp.dot(activated.astype(jnp.float32), weight_out.astype(jnp.float32), preferred_element_type=jnp.float32).astype(jnp.bfloat16)
        gate_weight = jnp.where(live_mask, flat_gates[picked], 0.0)
        return combined.at[token_ids].add(gate_weight[:, None] * expert_rows.astype(jnp.float32))
    combined = lax.fori_loop(0, EXPERTS, add_expert, jnp.zeros((TOKEN_COUNT, D), jnp.float32))
    layer_out = (residual_mid + combined).astype(jnp.bfloat16)
    return (mixer_out, layer_out)
```

```python
import functools

import jax
import jax.numpy as jnp
from jax import lax
from jax.experimental import pallas as pl
from jax.experimental.pallas import tpu as pltpu
from jax.sharding import PartitionSpec as P

HK = 8
VALUE_HEAD_SET = 16
DK = 128
DV = 128
MOE_H = 512
CONV = 4
TOPK = 3
TOK_DEV = 128
GROUP = VALUE_HEAD_SET // HK
HALO = 8
STEP_KEYS = 2

f32 = jnp.float32
bf16 = jnp.bfloat16
VMEM_LIMIT = 48 << 20


def round_up(value, multiple):
    return (value + multiple - 1) // multiple * multiple


def dot(lhs, rhs):
    return jnp.dot(lhs, rhs, preferred_element_type=f32)


def dot_nt(lhs, rhs):
    return lax.dot_general(lhs, rhs, (((1,), (1,)), ((), ())), preferred_element_type=f32)


def halves(value):
    high = value.astype(bf16)
    return high, (value - high.astype(f32)).astype(bf16)


def one_pass(lhs, rhs):
    return dot(lhs.astype(bf16), rhs.astype(bf16))


def three_pass(lhs, rhs):
    (lhs_high, lhs_low), (rhs_high, rhs_low) = halves(lhs), halves(rhs)
    return dot(lhs_high, rhs_high) + (dot(lhs_high, rhs_low) + dot(lhs_low, rhs_high))


def three_pass_nt(lhs, rhs):
    (lhs_high, lhs_low), (rhs_high, rhs_low) = lhs, rhs
    return dot_nt(lhs_high, rhs_high) + (dot_nt(lhs_high, rhs_low) + dot_nt(lhs_low, rhs_high))


def silu(value):
    return value * jax.nn.sigmoid(value)


def conv_silu(ref, halo_ref, weight_ref):
    rows = ref.shape[0]
    padded = jnp.concatenate([halo_ref[...].astype(f32), ref[...].astype(f32)], axis=0)
    total = padded[HALO:] * weight_ref[CONV - 1 : CONV, :]
    for tap in range(CONV - 1):
        start = HALO - (CONV - 1) + tap
        total = total + padded[start : start + rows] * weight_ref[tap : tap + 1, :]
    return silu(total)


def local_kernel(
    splits,
    part,
    part_rows,
    q_ref,
    k_ref,
    v_ref,
    qh_ref,
    kh_ref,
    vh_ref,
    qw_ref,
    kw_ref,
    vw_ref,
    beta_ref,
    decay_ref,
    send_ref,
    own_ref,
    reader_ref,
):
    rows = q_ref.shape[0]
    queries, keys, values = (
        conv_silu(q_ref, qh_ref, qw_ref),
        conv_silu(k_ref, kh_ref, kw_ref),
        conv_silu(v_ref, vh_ref, vw_ref),
    )
    row_ids = lax.broadcasted_iota(jnp.int32, (rows, rows), 0)
    col_ids = lax.broadcasted_iota(jnp.int32, (rows, rows), 1)
    strict, causal, diagonal = row_ids > col_ids, row_ids >= col_ids, row_ids == col_ids
    identity = jnp.where(diagonal, 1.0, 0.0).astype(f32)

    query_hats, key_hats, grams, scores_raw = [], [], [], []
    for key in range(STEP_KEYS):
        span = slice(key * DK, (key + 1) * DK)
        query, key_rows = queries[:, span], keys[:, span]
        query = (
            query
            * lax.rsqrt(jnp.sum(query * query, axis=1, keepdims=True) + 1e-06)
            * DK ** (-0.5)
        )
        key_rows = key_rows * lax.rsqrt(
            jnp.sum(key_rows * key_rows, axis=1, keepdims=True) + 1e-06
        )
        query_hats.append(query)
        key_hats.append(key_rows)
        query_parts, key_parts = halves(query), halves(key_rows)
        grams.append(three_pass_nt(key_parts, key_parts))
        scores_raw.append(three_pass_nt(query_parts, key_parts))

    heads = range(STEP_KEYS * GROUP)
    lower, betas, fades, tails, fadings, wholes = [], [], [], [], [], []
    for head in heads:
        key = head // GROUP
        beta_row = beta_ref[key, head % GROUP : head % GROUP + 1, :]
        decay_row = decay_ref[key, head % GROUP : head % GROUP + 1, :]
        beta_col = jnp.sum(jnp.where(diagonal, beta_row, 0.0), axis=1, keepdims=True)
        decay_col = jnp.sum(jnp.where(diagonal, decay_row, 0.0), axis=1, keepdims=True)
        cum_col = jnp.sum(jnp.where(causal, decay_row, 0.0), axis=1, keepdims=True)
        cum_row = jnp.sum(jnp.where(row_ids <= col_ids, decay_col, 0.0), axis=0, keepdims=True)
        last = jnp.sum(decay_row, axis=1, keepdims=True)
        fading = jnp.where(causal, jnp.exp(jnp.where(causal, cum_col - cum_row, 0.0)), 0.0)
        lower.append(jnp.where(strict, beta_col * fading * grams[key], 0.0))
        betas.append(beta_col)
        fades.append(jnp.exp(cum_col))
        tails.append(jnp.exp(jnp.minimum(last - cum_col, 0.0)))
        fadings.append(fading)

    solved = [
        jnp.where(row_ids // 2 == col_ids // 2, identity - lower[head], 0.0) for head in heads
    ]
    size = 2
    while size < rows:
        joins = (row_ids // (2 * size) == col_ids // (2 * size)) & (
            row_ids // size != col_ids // size
        )
        parts = [solved[head].astype(bf16) for head in heads]
        inner = [
            dot(parts[head], jnp.where(joins, lower[head], 0.0).astype(bf16)) for head in heads
        ]
        solved = [solved[head] - dot(inner[head].astype(bf16), parts[head]) for head in heads]
        size *= 2
    residues = [
        (identity - solved[head]) - three_pass(lower[head], solved[head]) for head in heads
    ]
    solved = [solved[head] + one_pass(solved[head], residues[head]) for head in heads]

    for head in heads:
        key = head // GROUP
        value_span = slice(head * DV, (head + 1) * DV)
        fresh_carried = three_pass(
            solved[head],
            jnp.concatenate(
                [
                    betas[head] * values[:, value_span],
                    (betas[head] * fades[head]) * key_hats[key],
                ],
                axis=1,
            ),
        )
        sums = three_pass(fresh_carried.T, tails[head] * key_hats[key])
        transition, state_add = sums[DV:], sums[:DV]
        for split in range(splits):
            send_ref[head, split, :DK, :] = transition.astype(bf16)
            added = state_add[split * part : (split + 1) * part].astype(bf16)
            if part == part_rows:
                send_ref[head, split, DK:, :] = added
            else:
                send_ref[head, split, DK:, :] = jnp.concatenate(
                    [added, jnp.zeros((part_rows - part, DK), bf16)], axis=0
                )
        mixed = three_pass(fadings[head] * scores_raw[key], fresh_carried)
        own_ref[head] = mixed[:, :DV]
        reader_ref[head] = fades[head] * query_hats[key] - mixed[:, DV:]


def local_terms(mixed_qkv, halo, conv_weight, beta, log_decay, splits, part_rows):
    rows = mixed_qkv.shape[0]
    key_cols, value_cols = STEP_KEYS * DK, STEP_KEYS * GROUP * DV
    steps = HK // STEP_KEYS
    value_from = 2 * HK * DK // value_cols
    part = DV // splits
    col_maps = (
        (key_cols, lambda i: (0, i)),
        (key_cols, lambda i: (0, steps + i)),
        (value_cols, lambda i: (0, value_from + i)),
    )
    specs = [
        pl.BlockSpec((height, width), index)
        for height in (rows, HALO, CONV)
        for width, index in col_maps
    ]
    per_head = pl.BlockSpec((STEP_KEYS, GROUP, rows), lambda i: (i, 0, 0))
    step_heads = STEP_KEYS * GROUP
    return pl.pallas_call(
        functools.partial(local_kernel, splits, part, part_rows),
        grid=(steps,),
        in_specs=specs + [per_head, per_head],
        out_specs=[
            pl.BlockSpec((step_heads, splits, DK + part_rows, DK), lambda i: (i, 0, 0, 0)),
            pl.BlockSpec((step_heads, rows, DV), lambda i: (i, 0, 0)),
            pl.BlockSpec((step_heads, rows, DK), lambda i: (i, 0, 0)),
        ],
        out_shape=[
            jax.ShapeDtypeStruct((VALUE_HEAD_SET, splits, DK + part_rows, DK), bf16),
            jax.ShapeDtypeStruct((VALUE_HEAD_SET, rows, DV), f32),
            jax.ShapeDtypeStruct((VALUE_HEAD_SET, rows, DK), f32),
        ],
        compiler_params=pltpu.CompilerParams(
            dimension_semantics=("arbitrary",), vmem_limit_bytes=VMEM_LIMIT
        ),
        name="local_terms",
    )(
        *[mixed_qkv] * 3,
        *[halo] * 3,
        *[conv_weight] * 3,
        beta.reshape(HK, GROUP, rows),
        log_decay.reshape(HK, GROUP, rows),
    )


def scan_kernel(fade_ref, sums_ref, start_ref, state_ref):
    step, block = pl.program_id(0), sums_ref.shape[0]

    @pl.when(step == 0)
    def _():
        state_ref[...] = jnp.zeros_like(state_ref)

    state = state_ref[...]
    for place in range(block):
        high, low = halves(state)
        start_ref[place] = high
        transition = sums_ref[place, :DK, :]
        moved = dot(high, transition) + dot(low, transition)
        added = sums_ref[place, DK:, :].astype(f32)
        state = (fade_ref[step * block + place] * state - moved) + added
    state_ref[...] = state


def scan_states(fade, sums):
    count, height = sums.shape[:2]
    part_rows = height - DK
    block = 8
    return pl.pallas_call(
        scan_kernel,
        grid_spec=pltpu.PrefetchScalarGridSpec(
            num_scalar_prefetch=1,
            grid=(count // block,),
            in_specs=[pl.BlockSpec((block, height, DK), lambda i, fade: (i, 0, 0))],
            out_specs=pl.BlockSpec((block, part_rows, DK), lambda i, fade: (i, 0, 0)),
            scratch_shapes=[pltpu.VMEM((part_rows, DK), f32)],
        ),
        out_shape=jax.ShapeDtypeStruct((count, part_rows, DK), bf16),
        compiler_params=pltpu.CompilerParams(
            dimension_semantics=("arbitrary",), vmem_limit_bytes=VMEM_LIMIT
        ),
        name="scan_states",
    )(fade, sums)


def route_kernel(capacity, routes_ref, gates_ref, select_ref, gather_ref):
    rows = routes_ref.shape[1]
    experts = select_ref.shape[0] // capacity
    expert_ids = lax.broadcasted_iota(jnp.int32, (experts, rows), 0)
    chosen = jnp.zeros((experts, rows), jnp.bool_)
    gates = jnp.zeros((experts, rows), f32)
    for choice in range(TOPK):
        named = routes_ref[choice : choice + 1, :] == expert_ids
        chosen = chosen | named
        gates = gates + jnp.where(named, gates_ref[choice : choice + 1, :], 0.0)
    earlier = lax.broadcasted_iota(jnp.int32, (rows, rows), 0) < lax.broadcasted_iota(
        jnp.int32, (rows, rows), 1
    )
    rank = dot(
        jnp.where(chosen, 1.0, 0.0).astype(bf16), jnp.where(earlier, 1.0, 0.0).astype(bf16)
    )
    slot = jnp.where(chosen, rank, -1.0).astype(jnp.int32)
    slot_ids = lax.broadcasted_iota(jnp.int32, (capacity, rows), 0)
    for expert in range(experts):
        span = slice(expert * capacity, (expert + 1) * capacity)
        taken = slot_ids == slot[expert : expert + 1, :]
        select_ref[span, :] = jnp.where(taken, 1.0, 0.0).astype(bf16)
        gather_ref[span, :] = jnp.where(taken, gates[expert : expert + 1, :], 0.0)


def route_tables(routes, route_gates, experts, capacity):
    rows = routes.shape[0]
    slots = experts * capacity
    return pl.pallas_call(
        functools.partial(route_kernel, capacity),
        out_shape=[
            jax.ShapeDtypeStruct((slots, rows), bf16),
            jax.ShapeDtypeStruct((slots, rows), f32),
        ],
        name="route_tables",
    )(routes.T, route_gates.T)


def mixer_kernel(
    own_ref,
    reader_ref,
    state_ref,
    gate_ref,
    resid_ref,
    head_gain_ref,
    moe_gain_ref,
    select_ref,
    mixer_ref,
    middle_ref,
    rows_ref,
):
    squares = None
    for head in range(VALUE_HEAD_SET):
        span = slice(head * DV, (head + 1) * DV)
        state = state_ref[head]
        high, low = halves(reader_ref[head])
        head_out = own_ref[head] + (dot_nt(high, state) + dot_nt(low, state))
        scaled = (
            head_out
            * lax.rsqrt(jnp.mean(head_out * head_out, axis=1, keepdims=True) + 1e-06)
            * head_gain_ref[...]
        )
        mixed = (scaled * silu(gate_ref[:, span].astype(f32))).astype(bf16)
        mixer_ref[:, span] = mixed
        middle = resid_ref[:, span].astype(f32) + mixed.astype(f32)
        middle_ref[:, span] = middle
        part = jnp.sum(middle * middle, axis=1, keepdims=True)
        squares = part if squares is None else squares + part
    width = resid_ref.shape[1]
    moe_input = (
        middle_ref[...] * lax.rsqrt(squares / width + 1e-06) * moe_gain_ref[...]
    ).astype(bf16)
    rows_ref[...] = dot(select_ref[...], moe_input).astype(bf16)


def mixer(own, reader, state, out_gate, resid, head_gain, moe_gain, select):
    rows, width = resid.shape
    return pl.pallas_call(
        mixer_kernel,
        out_shape=[
            jax.ShapeDtypeStruct((rows, width), bf16),
            jax.ShapeDtypeStruct((rows, width), f32),
            jax.ShapeDtypeStruct((select.shape[0], width), bf16),
        ],
        compiler_params=pltpu.CompilerParams(vmem_limit_bytes=VMEM_LIMIT),
        name="mixer",
    )(own, reader, state, out_gate, resid, head_gain[None], moe_gain[None], select)


def expert_kernel(rows_ref, win_ref, wout_ref, out_ref):
    projected = dot(rows_ref[...], win_ref[...])
    activated = (silu(projected[:, :MOE_H]) * projected[:, MOE_H:]).astype(bf16)
    cols = wout_ref.shape[2]
    for part in range(wout_ref.shape[0]):
        out_ref[:, part * cols : (part + 1) * cols] = dot(activated, wout_ref[part]).astype(bf16)


def expert_mlp(rows, whole_in, whole_out):
    count, width = rows.shape
    block = min(count, 256)
    return pl.pallas_call(
        expert_kernel,
        grid=(count // block,),
        in_specs=[
            pl.BlockSpec((block, width), lambda i: (i, 0)),
            pl.BlockSpec(whole_in.shape, lambda i: (0, 0)),
            pl.BlockSpec(whole_out.shape, lambda i: (0, 0, 0)),
        ],
        out_specs=pl.BlockSpec((block, width), lambda i: (i, 0)),
        out_shape=jax.ShapeDtypeStruct((count, width), bf16),
        compiler_params=pltpu.CompilerParams(
            dimension_semantics=("arbitrary",), vmem_limit_bytes=VMEM_LIMIT
        ),
        name="expert_mlp",
    )(rows, whole_in, whole_out)


def combine_kernel(gather_ref, rows_ref, middle_ref, out_ref):
    high, low = halves(gather_ref[...].T)
    out_ref[...] = (
        middle_ref[...] + (dot(high, rows_ref[...]) + dot(low, rows_ref[...]))
    ).astype(bf16)


def combine(gather, rows, middle):
    return pl.pallas_call(
        combine_kernel,
        out_shape=jax.ShapeDtypeStruct(middle.shape, bf16),
        compiler_params=pltpu.CompilerParams(vmem_limit_bytes=VMEM_LIMIT),
        name="combine",
    )(gather, rows, middle)


def shards(
    resid,
    mixed_qkv,
    out_gate,
    beta,
    log_decay,
    conv_weight,
    head_gain,
    moe_gain,
    routes,
    route_gates,
    w_in,
    w_out,
):
    every = ("ctx", "ep")
    count = lax.axis_size("ctx") * lax.axis_size("ep")
    experts = lax.axis_size("ep")
    splits = count // VALUE_HEAD_SET
    part = DV // splits
    part_rows = round_up(part, 16)
    capacity = round_up(
        max(2, (5 * TOK_DEV * TOPK + 4 * experts - 1) // (4 * experts)), 16
    )
    rows = mixed_qkv.shape[0]

    halo = lax.ppermute(
        mixed_qkv[rows - HALO :], every, [(source, source + 1) for source in range(count - 1)]
    )
    whole_in = lax.all_gather(w_in[0], "ctx", axis=0, tiled=True)
    whole_out = lax.all_gather(w_out[0], "ctx", axis=0)
    fades = lax.all_gather(jnp.exp(jnp.sum(log_decay, axis=1)), every)
    my_head = lax.axis_index(every) // splits
    fade = lax.dynamic_index_in_dim(fades, my_head, axis=1, keepdims=False)

    send, own, reader = local_terms(
        mixed_qkv, halo, conv_weight, beta, log_decay, splits, part_rows
    )
    sums = lax.all_to_all(
        send.reshape(count, DK + part_rows, DK), every, split_axis=0, concat_axis=0, tiled=True
    )
    starts = scan_states(fade, sums)
    states = lax.all_to_all(starts, every, split_axis=0, concat_axis=0, tiled=True)
    states = states[:, :part].reshape(VALUE_HEAD_SET, DV, DK)

    select, gather = route_tables(routes, route_gates, experts, capacity)
    mixer_out, middle, send_rows = mixer(
        own, reader, states, out_gate, resid, head_gain, moe_gain, select
    )
    expert_in = lax.all_to_all(send_rows, "ep", split_axis=0, concat_axis=0, tiled=True)
    expert_out = expert_mlp(expert_in, whole_in, whole_out)
    returned = lax.all_to_all(expert_out, "ep", split_axis=0, concat_axis=0, tiled=True)
    return mixer_out, combine(gather, returned, middle)


def solution(mesh):
    split_rows, split_cols = P(("ctx", "ep"), None), P(None, ("ctx", "ep"))
    return jax.shard_map(
        shards,
        mesh=mesh,
        in_specs=(
            split_rows,
            split_rows,
            split_rows,
            split_cols,
            split_cols,
            P(),
            P(),
            P(),
            split_rows,
            split_rows,
            P("ep", "ctx", None),
            P("ep", None, "ctx"),
        ),
        out_specs=(split_rows, split_rows),
        check_vma=False,
    )
```

```python
import functools

import jax
import jax.numpy as jnp
from jax import lax
from jax.experimental import pallas as pl
from jax.experimental.pallas import tpu as pltpu
from jax.sharding import Mesh
from jax.sharding import PartitionSpec as P

HK = 8
VALUE_HEAD_SET = 16
DK = 128
DV = 128
MOE_H = 512
CONV = 4
TOPK = 3
TOK_DEV = 128
GROUP = VALUE_HEAD_SET // HK
HALO = 8
STEP_KEYS = 2
FADE_ROWS = 16

f32 = jnp.float32
bf16 = jnp.bfloat16


def round_up(value, multiple):
    return (value + multiple - 1) // multiple * multiple


def hbm(*arrays):
    return [pltpu.with_memory_space_constraint(array, pltpu.HBM) for array in arrays]


def dot(lhs, rhs):
    return jnp.dot(lhs, rhs, preferred_element_type=f32)


def dot_nt(lhs, rhs):
    return lax.dot_general(lhs, rhs, (((1,), (1,)), ((), ())), preferred_element_type=f32)


def halves(value):
    high = value.astype(bf16)
    return high, (value - high.astype(f32)).astype(bf16)


def one_pass(lhs, rhs):
    return dot(lhs.astype(bf16), rhs.astype(bf16))


def three_pass(lhs, rhs):
    (lhs_high, lhs_low), (rhs_high, rhs_low) = halves(lhs), halves(rhs)
    return dot(lhs_high, rhs_high) + (dot(lhs_high, rhs_low) + dot(lhs_low, rhs_high))


def three_pass_nt(lhs, rhs):
    (lhs_high, lhs_low), (rhs_high, rhs_low) = lhs, rhs
    return dot_nt(lhs_high, rhs_high) + (dot_nt(lhs_high, rhs_low) + dot_nt(lhs_low, rhs_high))


def silu(value):
    return value * jax.nn.sigmoid(value)


def conv_silu(ref, halo_ref, weight_ref):
    rows = ref.shape[0]
    padded = jnp.concatenate([halo_ref[...].astype(f32), ref[...].astype(f32)], axis=0)
    total = padded[HALO:] * weight_ref[CONV - 1 : CONV, :]
    for tap in range(CONV - 1):
        start = HALO - (CONV - 1) + tap
        total = total + padded[start : start + rows] * weight_ref[tap : tap + 1, :]
    return silu(total)


def fade_tile(fade):
    left = jnp.broadcast_to(fade, (FADE_ROWS, DK))
    row_ids = lax.broadcasted_iota(jnp.int32, (FADE_ROWS, DK), 0)
    tile = jnp.zeros((FADE_ROWS, DK), f32)
    for term in range(3):
        part = left.astype(bf16).astype(f32)
        tile = jnp.where(row_ids == term, part, tile)
        left = left - part
    return tile.astype(bf16)


def key_rows_hat(key_rows):
    return key_rows * lax.rsqrt(jnp.sum(key_rows * key_rows, axis=1, keepdims=True) + 1e-06)


def decay_terms(decay_row, masks):
    diagonal, causal, upper = masks
    decay_col = jnp.sum(jnp.where(diagonal, decay_row, 0.0), axis=1, keepdims=True)
    cum_col = jnp.sum(jnp.where(causal, decay_row, 0.0), axis=1, keepdims=True)
    cum_row = jnp.sum(jnp.where(upper, decay_col, 0.0), axis=0, keepdims=True)
    fading = jnp.where(causal, jnp.exp(jnp.where(causal, cum_col - cum_row, 0.0)), 0.0)
    return cum_col, fading


def square_ids(rows):
    return (
        lax.broadcasted_iota(jnp.int32, (rows, rows), 0),
        lax.broadcasted_iota(jnp.int32, (rows, rows), 1),
    )


def local_kernel(
    splits,
    part,
    part_rows,
    k_ref,
    v_ref,
    kh_ref,
    vh_ref,
    kw_ref,
    vw_ref,
    beta_ref,
    decay_ref,
    send_ref,
    hat_ref,
    fresh_ref,
):
    rows = k_ref.shape[0]
    keys, values = conv_silu(k_ref, kh_ref, kw_ref), conv_silu(v_ref, vh_ref, vw_ref)
    row_ids, col_ids = square_ids(rows)
    strict, causal, diagonal = row_ids > col_ids, row_ids >= col_ids, row_ids == col_ids
    masks = diagonal, causal, row_ids <= col_ids
    identity = jnp.where(diagonal, 1.0, 0.0).astype(f32)

    key_hats, grams = [], []
    for key in range(STEP_KEYS):
        key_hat = key_rows_hat(keys[:, key * DK : (key + 1) * DK])
        hat_ref[key] = key_hat
        key_hats.append(key_hat)
        parts = halves(key_hat)
        grams.append(three_pass_nt(parts, parts))

    heads = range(STEP_KEYS * GROUP)
    lower, betas, fades, tails, wholes = [], [], [], [], []
    for head in heads:
        key, member = head // GROUP, head % GROUP
        beta_row = beta_ref[key, member : member + 1, :]
        decay_row = decay_ref[key, member : member + 1, :]
        beta_col = jnp.sum(jnp.where(diagonal, beta_row, 0.0), axis=1, keepdims=True)
        cum_col, fading = decay_terms(decay_row, masks)
        last = jnp.sum(decay_row, axis=1, keepdims=True)
        lower.append(jnp.where(strict, beta_col * fading * grams[key], 0.0))
        betas.append(beta_col)
        fades.append(jnp.exp(cum_col))
        tails.append(jnp.exp(jnp.minimum(last - cum_col, 0.0)))
        wholes.append(jnp.exp(last))

    solved = [
        jnp.where(row_ids // 2 == col_ids // 2, identity - lower[head], 0.0) for head in heads
    ]
    size = 2
    while size < rows:
        joins = (row_ids // (2 * size) == col_ids // (2 * size)) & (
            row_ids // size != col_ids // size
        )
        parts = [solved[head].astype(bf16) for head in heads]
        inner = [
            dot(parts[head], jnp.where(joins, lower[head], 0.0).astype(bf16)) for head in heads
        ]
        solved = [solved[head] - dot(inner[head].astype(bf16), parts[head]) for head in heads]
        size *= 2
    residues = [
        (identity - solved[head]) - three_pass(lower[head], solved[head]) for head in heads
    ]
    solved = [solved[head] + one_pass(solved[head], residues[head]) for head in heads]

    for head in heads:
        key = head // GROUP
        value_span = slice(head * DV, (head + 1) * DV)
        fresh_carried = three_pass(
            solved[head],
            jnp.concatenate(
                [
                    betas[head] * values[:, value_span],
                    (betas[head] * fades[head]) * key_hats[key],
                ],
                axis=1,
            ),
        )
        fresh_ref[head] = fresh_carried
        sums = three_pass(fresh_carried.T, tails[head] * key_hats[key])
        transition, state_add = sums[DV:].astype(bf16), sums[:DV].astype(bf16)
        fade_rows = fade_tile(wholes[head])
        for split in range(splits):
            send_ref[head, split, :DK, :] = transition
            for core in range(2):
                place = 2 * split + core
                added = state_add[place * part : (place + 1) * part]
                if part < part_rows:
                    added = jnp.concatenate(
                        [added, jnp.zeros((part_rows - part, DK), bf16)], axis=0
                    )
                send_ref[head, split, pl.ds(DK + core * part_rows, part_rows), :] = added
            send_ref[head, split, pl.ds(DK + 2 * part_rows, FADE_ROWS), :] = fade_rows


def local_terms(mixed_qkv, halo, conv_weight, beta, log_decay, splits, part, part_rows):
    rows = mixed_qkv.shape[0]
    key_cols, value_cols = STEP_KEYS * DK, STEP_KEYS * GROUP * DV
    steps = HK // STEP_KEYS
    value_from = 2 * HK * DK // value_cols
    height = DK + 2 * part_rows + FADE_ROWS
    col_maps = (
        (key_cols, lambda i: (0, steps + i)),
        (value_cols, lambda i: (0, value_from + i)),
    )
    specs = [
        pl.BlockSpec((tall, width), index)
        for tall in (rows, HALO, CONV)
        for width, index in col_maps
    ]
    per_key = pl.BlockSpec((STEP_KEYS, GROUP, rows), lambda i: (i, 0, 0))
    step_heads = STEP_KEYS * GROUP
    return pl.pallas_call(
        functools.partial(local_kernel, splits, part, part_rows),
        grid=(steps,),
        in_specs=specs + [per_key, per_key],
        out_specs=[
            pl.BlockSpec((step_heads, splits, height, DK), lambda i: (i, 0, 0, 0)),
            pl.BlockSpec((STEP_KEYS, rows, DK), lambda i: (i, 0, 0)),
            pl.BlockSpec((step_heads, rows, DV + DK), lambda i: (i, 0, 0)),
        ],
        out_shape=[
            pltpu.HBM((VALUE_HEAD_SET, splits, height, DK), bf16),
            pltpu.HBM((HK, rows, DK), f32),
            pltpu.HBM((VALUE_HEAD_SET, rows, DV + DK), f32),
        ],
        compiler_params=pltpu.CompilerParams(
            dimension_semantics=("arbitrary",), vmem_limit_bytes=24 << 20
        ),
        name="local_terms",
    )(
        *hbm(mixed_qkv, mixed_qkv),
        halo,
        halo,
        *hbm(conv_weight, conv_weight, beta, log_decay),
    )


def reader_kernel(
    q_ref, qh_ref, qw_ref, hat_ref, decay_ref, fresh_ref, own_ref, reader_ref
):
    rows = q_ref.shape[0]
    queries = conv_silu(q_ref, qh_ref, qw_ref)
    row_ids, col_ids = square_ids(rows)
    masks = row_ids == col_ids, row_ids >= col_ids, row_ids <= col_ids
    for key in range(STEP_KEYS):
        query = key_rows_hat(queries[:, key * DK : (key + 1) * DK]) * DK ** (-0.5)
        raw = three_pass_nt(halves(query), halves(hat_ref[key]))
        for member in range(GROUP):
            head = key * GROUP + member
            cum_col, fading = decay_terms(decay_ref[key, member : member + 1, :], masks)
            mixed = three_pass(fading * raw, fresh_ref[head])
            own_ref[head] = mixed[:, :DV]
            reader_ref[head] = jnp.exp(cum_col) * query - mixed[:, DV:]


def reader_terms(mixed_qkv, halo, conv_weight, log_decay, hats, fresh):
    rows = mixed_qkv.shape[0]
    key_cols, step_heads = STEP_KEYS * DK, STEP_KEYS * GROUP
    per_head = pl.BlockSpec((step_heads, rows, DK), lambda i: (i, 0, 0))
    return pl.pallas_call(
        reader_kernel,
        grid=(HK // STEP_KEYS,),
        in_specs=[pl.BlockSpec((tall, key_cols), lambda i: (0, i)) for tall in (rows, HALO, CONV)]
        + [
            pl.BlockSpec((STEP_KEYS, rows, DK), lambda i: (i, 0, 0)),
            pl.BlockSpec((STEP_KEYS, GROUP, rows), lambda i: (i, 0, 0)),
            pl.BlockSpec((step_heads, rows, DV + DK), lambda i: (i, 0, 0)),
        ],
        out_specs=[per_head, per_head],
        out_shape=[pltpu.HBM((VALUE_HEAD_SET, rows, DK), f32)] * 2,
        compiler_params=pltpu.CompilerParams(
            dimension_semantics=("arbitrary",), vmem_limit_bytes=24 << 20
        ),
        name="reader_terms",
    )(*hbm(mixed_qkv), halo, *hbm(conv_weight, hats, log_decay, fresh))


def scan_kernel(core_ref, near_ref, far_ref, start_ref, state_ref):
    step, core = pl.program_id(0), core_ref[0]
    block, part_rows = start_ref.shape[:2]

    @pl.when(step == 0)
    def _():
        state_ref[...] = jnp.zeros_like(state_ref)

    is_near = step % 2 == core
    added_at = pl.multiple_of(DK + core * part_rows, 16)
    state = state_ref[...]
    for place in range(block):

        def pick(span):
            return jnp.where(is_near, near_ref[place, span, :], far_ref[place, span, :])

        high, low = halves(state)
        start_ref[place] = high
        transition = pick(slice(0, DK))
        moved = dot(high, transition) + dot(low, transition)
        added = pick(pl.ds(added_at, part_rows)).astype(f32)
        terms = pick(slice(DK + 2 * part_rows, DK + 2 * part_rows + FADE_ROWS)).astype(f32)
        fade = terms[0:1] + (terms[1:2] + terms[2:3])
        state = (fade * state - moved) + added
    state_ref[...] = state


def scan_states(core, near, far, block, part_rows):
    chips, height = near.shape[:2]
    both = pl.BlockSpec((block, height, DK), lambda i, core: (i // 2, 0, 0))
    return pl.pallas_call(
        scan_kernel,
        grid_spec=pltpu.PrefetchScalarGridSpec(
            num_scalar_prefetch=1,
            grid=(2 * chips // block,),
            in_specs=[both, both],
            out_specs=pl.BlockSpec((block, part_rows, DK), lambda i, core: (i, 0, 0)),
            scratch_shapes=[pltpu.VMEM((part_rows, DK), f32)],
        ),
        out_shape=pltpu.HBM((2 * chips, part_rows, DK), bf16),
        compiler_params=pltpu.CompilerParams(
            dimension_semantics=("arbitrary",), vmem_limit_bytes=16 << 20
        ),
        name="scan_states",
    )(core, near, far)


def route_kernel(capacity, routes_ref, gates_ref, select_ref, gather_ref):
    rows = routes_ref.shape[1]
    experts = select_ref.shape[0] // capacity
    expert_ids = lax.broadcasted_iota(jnp.int32, (experts, rows), 0)
    chosen = jnp.zeros((experts, rows), jnp.bool_)
    gates = jnp.zeros((experts, rows), f32)
    for choice in range(TOPK):
        named = routes_ref[choice : choice + 1, :] == expert_ids
        chosen = chosen | named
        gates = gates + jnp.where(named, gates_ref[choice : choice + 1, :], 0.0)
    earlier = lax.broadcasted_iota(jnp.int32, (rows, rows), 0) < lax.broadcasted_iota(
        jnp.int32, (rows, rows), 1
    )
    rank = dot(
        jnp.where(chosen, 1.0, 0.0).astype(bf16), jnp.where(earlier, 1.0, 0.0).astype(bf16)
    )
    slot = jnp.where(chosen, rank, -1.0).astype(jnp.int32)
    slot_ids = lax.broadcasted_iota(jnp.int32, (capacity, rows), 0)
    for expert in range(experts):
        span = slice(expert * capacity, (expert + 1) * capacity)
        taken = slot_ids == slot[expert : expert + 1, :]
        select_ref[span, :] = jnp.where(taken, 1.0, 0.0).astype(bf16)
        gather_ref[span, :] = jnp.where(taken, gates[expert : expert + 1, :], 0.0)


def route_tables(routes, route_gates, experts, capacity):
    rows = routes.shape[0]
    slots = experts * capacity
    return pl.pallas_call(
        functools.partial(route_kernel, capacity),
        out_shape=[
            jax.ShapeDtypeStruct((slots, rows), bf16),
            jax.ShapeDtypeStruct((slots, rows), f32),
        ],
        name="route_tables",
    )(routes.T, route_gates.T)


def mixer_kernel(
    own_ref,
    reader_ref,
    state_ref,
    gate_ref,
    resid_ref,
    head_gain_ref,
    moe_gain_ref,
    select_ref,
    mixer_ref,
    middle_ref,
    rows_ref,
    squares_ref,
):
    step, heads = pl.program_id(0), own_ref.shape[0]
    squares = jnp.where(step == 0, jnp.zeros_like(squares_ref), squares_ref[...])
    for head in range(heads):
        span = slice(head * DV, (head + 1) * DV)
        if len(state_ref.shape) == 3:
            state = state_ref[head]
        else:
            state = jnp.concatenate([state_ref[0, core, head] for core in range(2)], axis=0)
        high, low = halves(reader_ref[head])
        head_out = own_ref[head] + (dot_nt(high, state) + dot_nt(low, state))
        scaled = (
            head_out
            * lax.rsqrt(jnp.mean(head_out * head_out, axis=1, keepdims=True) + 1e-06)
            * head_gain_ref[...]
        )
        mixed = (scaled * silu(gate_ref[:, span].astype(f32))).astype(bf16)
        mixer_ref[:, span] = mixed
        middle = resid_ref[:, span].astype(f32) + mixed.astype(f32)
        middle_ref[step * heads + head] = middle
        squares = squares + jnp.sum(middle * middle, axis=1, keepdims=True)
    squares_ref[...] = squares

    @pl.when(step == pl.num_programs(0) - 1)
    def _():
        scale = lax.rsqrt(squares / moe_gain_ref.shape[1] + 1e-06)
        select = select_ref[...]
        for head in range(VALUE_HEAD_SET):
            span = slice(head * DV, (head + 1) * DV)
            moe_input = (middle_ref[head] * scale * moe_gain_ref[:, span]).astype(bf16)
            rows_ref[:, span] = dot(select, moe_input).astype(bf16)


def mixer(own, reader, state, out_gate, resid, head_gain, moe_gain, select):
    rows, width = resid.shape
    heads = 4
    per_head = pl.BlockSpec((heads, rows, DV), lambda i: (i, 0, 0))
    columns = pl.BlockSpec((rows, heads * DV), lambda i: (0, i))
    if state.ndim == 3:
        state_spec = pl.BlockSpec((heads, DV, DK), lambda i: (i, 0, 0))
    else:
        block = state.shape[2] // heads
        state_spec = pl.BlockSpec(
            (1, 2, heads) + state.shape[3:], lambda i: (i // block, 0, i % block, 0, 0)
        )

    def whole(*shape):
        return pl.BlockSpec(shape, lambda i: (0,) * len(shape))

    return pl.pallas_call(
        mixer_kernel,
        grid=(VALUE_HEAD_SET // heads,),
        in_specs=[
            per_head,
            per_head,
            state_spec,
            columns,
            columns,
            whole(1, DV),
            whole(1, width),
            whole(*select.shape),
        ],
        out_specs=[
            columns,
            whole(VALUE_HEAD_SET, rows, DV),
            whole(select.shape[0], width),
        ],
        out_shape=[
            pltpu.HBM((rows, width), bf16),
            jax.ShapeDtypeStruct((VALUE_HEAD_SET, rows, DV), f32),
            pltpu.HBM((select.shape[0], width), bf16),
        ],
        scratch_shapes=[pltpu.VMEM((rows, 1), f32)],
        compiler_params=pltpu.CompilerParams(
            dimension_semantics=("arbitrary",), vmem_limit_bytes=24 << 20
        ),
        name="mixer",
    )(
        *hbm(own, reader),
        state,
        *hbm(out_gate, resid),
        head_gain[None],
        moe_gain[None],
        *hbm(select),
    )


def expert_in_kernel(order_ref, rows_ref, *refs):
    in_refs, result_ref = refs[:-1], refs[-1]
    projected = None
    for place, ref in enumerate(in_refs):
        depth = ref.shape[0]
        start = pl.multiple_of(order_ref[place] * depth, depth)
        term = dot(rows_ref[:, pl.ds(start, depth)], ref[...])
        projected = term if projected is None else projected + term
    result_ref[...] = (silu(projected[:, :MOE_H]) * projected[:, MOE_H:]).astype(bf16)


def expert_out_kernel(order_ref, activated_ref, *refs):
    out_refs, result_ref = refs[:-1], refs[-1]
    activated = activated_ref[...]
    for place, ref in enumerate(out_refs):
        cols = ref.shape[1]
        start = pl.multiple_of(order_ref[place] * cols, cols)
        result_ref[:, pl.ds(start, cols)] = dot(activated, ref[...]).astype(bf16)


def expert_call(kernel, name, order, rows, parts, width):
    count = rows.shape[0]
    block = min(count, 256)
    return pl.pallas_call(
        kernel,
        grid_spec=pltpu.PrefetchScalarGridSpec(
            num_scalar_prefetch=1,
            grid=(count // block,),
            in_specs=[pl.BlockSpec((block, rows.shape[1]), lambda i, order: (i, 0))]
            + [pl.BlockSpec(part.shape, lambda i, order: (0, 0)) for part in parts],
            out_specs=pl.BlockSpec((block, width), lambda i, order: (i, 0)),
        ),
        out_shape=jax.ShapeDtypeStruct((count, width), bf16),
        compiler_params=pltpu.CompilerParams(
            dimension_semantics=("arbitrary",), vmem_limit_bytes=24 << 20
        ),
        name=name,
    )(order, rows, *hbm(*parts))


def expert_in(order, rows, parts):
    rows = rows.reshape(-1, rows.shape[-1])
    return expert_call(expert_in_kernel, "expert_in", order, rows, parts, MOE_H)


def expert_out(order, activated, parts, width):
    return expert_call(expert_out_kernel, "expert_out", order, activated, parts, width)


def combine_kernel(gather_ref, rows_ref, middle_ref, out_ref):
    high, low = halves(gather_ref[...].T)
    for head in range(middle_ref.shape[0]):
        span = slice(head * DV, (head + 1) * DV)
        rows = rows_ref[:, span]
        out_ref[:, span] = (middle_ref[head] + (dot(high, rows) + dot(low, rows))).astype(bf16)


def combine(gather, rows, middle):
    count, width = middle.shape[1], rows.shape[1]
    return pl.pallas_call(
        combine_kernel,
        out_shape=pltpu.HBM((count, width), bf16),
        compiler_params=pltpu.CompilerParams(vmem_limit_bytes=24 << 20),
        name="combine",
    )(gather, rows, middle)


def after(value, earlier):
    return lax.optimization_barrier((value, earlier))[0]


def across_halves(value, flip):
    pairs = [
        (core * 2 + half, half * 2 + (core ^ flip)) for core in range(2) for half in range(2)
    ]
    return lax.ppermute(value, ("core", "half"), pairs)


def along_y(value, y_count):
    moved = [value]
    for shift in range(1, y_count):
        pairs = [(source, (source + shift) % y_count) for source in range(y_count)]
        moved.append(lax.ppermute(value, "y", pairs))
    return moved


def shards(
    resid,
    mixed_qkv,
    out_gate,
    beta,
    log_decay,
    conv_weight,
    head_gain,
    moe_gain,
    routes,
    route_gates,
    w_in,
    w_out,
):
    every = ("y", "core", "half", "rest")
    y_count, rest_count = lax.axis_size("y"), lax.axis_size("rest")
    count = lax.axis_size(every)
    experts = 2 * rest_count
    chips, block = count // 2, 2 * rest_count
    splits = chips // VALUE_HEAD_SET
    part = DV // (2 * splits)
    part_rows = round_up(part, 16)
    capacity = round_up(
        max(2, (5 * TOK_DEV * TOPK + 4 * experts - 1) // (4 * experts)), 16
    )
    rows = mixed_qkv.shape[0]
    beta, log_decay = (value.reshape(HK, GROUP, rows) for value in (beta, log_decay))
    tie = lax.optimization_barrier

    halo = lax.ppermute(
        mixed_qkv[rows - HALO :], every, [(source, source + 1) for source in range(count - 1)]
    )
    in_first = across_halves(after(w_in[0], halo), 0)
    send, hats, fresh = local_terms(
        mixed_qkv, halo, conv_weight, beta, log_decay, splits, part, part_rows
    )

    near = lax.all_to_all(
        send.reshape(chips, -1, DK),
        ("y", "half", "rest"),
        split_axis=0,
        concat_axis=0,
        tiled=True,
    )
    hats, in_first = tie((hats, in_first))
    own, reader = reader_terms(mixed_qkv, halo, conv_weight, log_decay, hats, fresh)
    select, gather = route_tables(routes, route_gates, experts, capacity)
    in_first = along_y(after(in_first, own), y_count)
    out_first = across_halves(after(w_out[0], send), 0)
    near, in_first, out_first, own, reader, select = tie(
        (near, in_first, out_first, own, reader, select)
    )

    in_second = across_halves(after(w_in[0], near), 1)
    far = lax.ppermute(near, "core", [(0, 1), (1, 0)])
    core = lax.axis_index("core").astype(jnp.int32).reshape(1)
    starts = scan_states(core, near, far, block, part_rows)
    states = lax.all_to_all(starts, every, split_axis=0, concat_axis=0, tiled=True)
    out_first = along_y(out_first, y_count)
    states, in_second, out_first = tie((states, in_second, out_first))

    states = states.reshape(y_count, 2, block, part_rows, DK)
    if part < part_rows or splits > 1:
        states = states[:, :, :, :part].transpose(0, 2, 1, 3, 4)
        states = states.reshape(VALUE_HEAD_SET, DV, DK)
    mixer_out, middle, send_rows = mixer(
        own, reader, states, out_gate, resid, head_gain, moe_gain, select
    )
    in_second = along_y(after(in_second, send_rows), y_count)
    out_second = across_halves(after(w_out[0], send_rows), 1)
    out_second = along_y(out_second, y_count)
    exchange = functools.partial(
        lax.all_to_all, axis_name=("core", "rest"), split_axis=0, concat_axis=0, tiled=True
    )
    y_index, half = lax.axis_index("y"), lax.axis_index("half")
    order = jnp.stack(
        [
            (y_index - shift) % y_count * 2 + (half ^ flip)
            for flip in range(2)
            for shift in range(y_count)
        ]
    )
    activated = expert_in(order, exchange(send_rows), in_first + in_second)
    expert_rows = expert_out(order, activated, out_first + out_second, send_rows.shape[1])
    return mixer_out, combine(gather, exchange(expert_rows), middle)


def solution(mesh):
    ctx_count, ep_count = mesh.shape["ctx"], mesh.shape["ep"]
    names = ("y", "core", "half", "rest")
    fine = Mesh(mesh.devices.reshape(ctx_count // 2, 2, 2, ep_count // 2), names)
    split_rows, split_cols = P(names, None), P(None, names)
    ctx, ep = names[:2], names[2:]
    return jax.shard_map(
        shards,
        mesh=fine,
        in_specs=(
            split_rows,
            split_rows,
            split_rows,
            split_cols,
            split_cols,
            P(),
            P(),
            P(),
            split_rows,
            split_rows,
            P(ep, ctx, None),
            P(ep, None, ctx),
        ),
        out_specs=(split_rows, split_rows),
        check_vma=False,
    )
```

```python
import functools

import jax
import jax.numpy as jnp
from jax import lax
from jax.experimental import pallas as pl
from jax.experimental.pallas import tpu as pltpu
from jax.sharding import Mesh
from jax.sharding import PartitionSpec as P

HK = 8
VALUE_HEAD_SET = 16
DK = 128
DV = 128
MOE_H = 512
CONV = 4
TOPK = 3
TOK_DEV = 128
GROUP = VALUE_HEAD_SET // HK
HALO = 8
STEP_KEYS = 2
READER_KEYS = 2
FADE_ROWS = 16

f32 = jnp.float32
bf16 = jnp.bfloat16


def round_up(value, multiple):
    return (value + multiple - 1) // multiple * multiple


def hbm(*arrays):
    return [pltpu.with_memory_space_constraint(array, pltpu.HBM) for array in arrays]


def dot(lhs, rhs):
    return jnp.dot(lhs, rhs, preferred_element_type=f32)


def dot_nt(lhs, rhs):
    return lax.dot_general(lhs, rhs, (((1,), (1,)), ((), ())), preferred_element_type=f32)


def halves(value):
    high = value.astype(bf16)
    return high, (value - high.astype(f32)).astype(bf16)


def one_pass(lhs, rhs):
    return dot(lhs.astype(bf16), rhs.astype(bf16))


def three_pass(lhs, rhs):
    (lhs_high, lhs_low), (rhs_high, rhs_low) = halves(lhs), halves(rhs)
    return dot(lhs_high, rhs_high) + (dot(lhs_high, rhs_low) + dot(lhs_low, rhs_high))


def three_pass_nt(lhs, rhs):
    (lhs_high, lhs_low), (rhs_high, rhs_low) = lhs, rhs
    return dot_nt(lhs_high, rhs_high) + (dot_nt(lhs_high, rhs_low) + dot_nt(lhs_low, rhs_high))


def silu(value):
    return value * jax.nn.sigmoid(value)


def conv_silu(ref, halo_ref, weight_ref):
    rows = ref.shape[0]
    padded = jnp.concatenate([halo_ref[...].astype(f32), ref[...].astype(f32)], axis=0)
    total = padded[HALO:] * weight_ref[CONV - 1 : CONV, :]
    for tap in range(CONV - 1):
        start = HALO - (CONV - 1) + tap
        total = total + padded[start : start + rows] * weight_ref[tap : tap + 1, :]
    return silu(total)


def fade_tile(fade):
    left = jnp.broadcast_to(fade, (FADE_ROWS, DK))
    row_ids = lax.broadcasted_iota(jnp.int32, (FADE_ROWS, DK), 0)
    tile = jnp.zeros((FADE_ROWS, DK), f32)
    for term in range(3):
        part = left.astype(bf16).astype(f32)
        tile = jnp.where(row_ids == term, part, tile)
        left = left - part
    return tile.astype(bf16)


def key_rows_hat(key_rows):
    return key_rows * lax.rsqrt(jnp.sum(key_rows * key_rows, axis=1, keepdims=True) + 1e-06)


def decay_terms(decay_row, masks):
    diagonal, causal, upper = masks
    decay_col = jnp.sum(jnp.where(diagonal, decay_row, 0.0), axis=1, keepdims=True)
    cum_col = jnp.sum(jnp.where(causal, decay_row, 0.0), axis=1, keepdims=True)
    cum_row = jnp.sum(jnp.where(upper, decay_col, 0.0), axis=0, keepdims=True)
    fading = jnp.where(causal, jnp.exp(jnp.where(causal, cum_col - cum_row, 0.0)), 0.0)
    return cum_col, fading


def square_ids(rows):
    return (
        lax.broadcasted_iota(jnp.int32, (rows, rows), 0),
        lax.broadcasted_iota(jnp.int32, (rows, rows), 1),
    )


def local_kernel(
    splits,
    part,
    part_rows,
    k_ref,
    v_ref,
    kh_ref,
    vh_ref,
    kw_ref,
    vw_ref,
    beta_ref,
    decay_ref,
    send_ref,
    hat_ref,
    fresh_ref,
):
    rows = k_ref.shape[0]
    keys, values = conv_silu(k_ref, kh_ref, kw_ref), conv_silu(v_ref, vh_ref, vw_ref)
    row_ids, col_ids = square_ids(rows)
    strict, causal, diagonal = row_ids > col_ids, row_ids >= col_ids, row_ids == col_ids
    masks = diagonal, causal, row_ids <= col_ids
    identity = jnp.where(diagonal, 1.0, 0.0).astype(f32)

    key_hats, grams = [], []
    for key in range(STEP_KEYS):
        key_hat = key_rows_hat(keys[:, key * DK : (key + 1) * DK])
        hat_ref[key] = key_hat
        key_hats.append(key_hat)
        parts = halves(key_hat)
        grams.append(three_pass_nt(parts, parts))

    heads = range(STEP_KEYS * GROUP)
    lower, betas, fades, tails, wholes = [], [], [], [], []
    for head in heads:
        key, member = head // GROUP, head % GROUP
        beta_row = beta_ref[key, member : member + 1, :]
        decay_row = decay_ref[key, member : member + 1, :]
        beta_col = jnp.sum(jnp.where(diagonal, beta_row, 0.0), axis=1, keepdims=True)
        cum_col, fading = decay_terms(decay_row, masks)
        last = jnp.sum(decay_row, axis=1, keepdims=True)
        lower.append(jnp.where(strict, beta_col * fading * grams[key], 0.0))
        betas.append(beta_col)
        fades.append(jnp.exp(cum_col))
        tails.append(jnp.exp(jnp.minimum(last - cum_col, 0.0)))
        wholes.append(jnp.exp(last))

    solved = [
        jnp.where(row_ids // 2 == col_ids // 2, identity - lower[head], 0.0) for head in heads
    ]
    size = 2
    while size < rows:
        joins = (row_ids // (2 * size) == col_ids // (2 * size)) & (
            row_ids // size != col_ids // size
        )
        parts = [solved[head].astype(bf16) for head in heads]
        inner = [
            dot(parts[head], jnp.where(joins, lower[head], 0.0).astype(bf16)) for head in heads
        ]
        solved = [solved[head] - dot(inner[head].astype(bf16), parts[head]) for head in heads]
        size *= 2
    residues = [
        (identity - solved[head]) - three_pass(lower[head], solved[head]) for head in heads
    ]
    solved = [solved[head] + one_pass(solved[head], residues[head]) for head in heads]

    for head in heads:
        key = head // GROUP
        value_span = slice(head * DV, (head + 1) * DV)
        fresh_carried = three_pass(
            solved[head],
            jnp.concatenate(
                [
                    betas[head] * values[:, value_span],
                    (betas[head] * fades[head]) * key_hats[key],
                ],
                axis=1,
            ),
        )
        fresh_ref[head] = fresh_carried
        sums = three_pass(fresh_carried.T, tails[head] * key_hats[key])
        transition, state_add = sums[DV:].astype(bf16), sums[:DV].astype(bf16)
        fade_rows = fade_tile(wholes[head])
        for split in range(splits):
            send_ref[head, split, :DK, :] = transition
            for core in range(2):
                place = 2 * split + core
                added = state_add[place * part : (place + 1) * part]
                if part < part_rows:
                    added = jnp.concatenate(
                        [added, jnp.zeros((part_rows - part, DK), bf16)], axis=0
                    )
                send_ref[head, split, pl.ds(DK + core * part_rows, part_rows), :] = added
            send_ref[head, split, pl.ds(DK + 2 * part_rows, FADE_ROWS), :] = fade_rows


def local_terms(mixed_qkv, halo, conv_weight, beta, log_decay, splits, part, part_rows):
    rows = mixed_qkv.shape[0]
    key_cols, value_cols = STEP_KEYS * DK, STEP_KEYS * GROUP * DV
    steps = HK // STEP_KEYS
    value_from = 2 * HK * DK // value_cols
    height = DK + 2 * part_rows + FADE_ROWS
    col_maps = (
        (key_cols, lambda i: (0, steps + i)),
        (value_cols, lambda i: (0, value_from + i)),
    )
    specs = [
        pl.BlockSpec((tall, width), index)
        for tall in (rows, HALO, CONV)
        for width, index in col_maps
    ]
    per_key = pl.BlockSpec((STEP_KEYS, GROUP, rows), lambda i: (i, 0, 0))
    step_heads = STEP_KEYS * GROUP
    return pl.pallas_call(
        functools.partial(local_kernel, splits, part, part_rows),
        grid=(steps,),
        in_specs=specs + [per_key, per_key],
        out_specs=[
            pl.BlockSpec((step_heads, splits, height, DK), lambda i: (i, 0, 0, 0)),
            pl.BlockSpec((STEP_KEYS, rows, DK), lambda i: (i, 0, 0)),
            pl.BlockSpec((step_heads, rows, DV + DK), lambda i: (i, 0, 0)),
        ],
        out_shape=[
            pltpu.HBM((VALUE_HEAD_SET, splits, height, DK), bf16),
            pltpu.HBM((HK, rows, DK), f32),
            pltpu.HBM((VALUE_HEAD_SET, rows, DV + DK), f32),
        ],
        compiler_params=pltpu.CompilerParams(
            dimension_semantics=("arbitrary",), vmem_limit_bytes=24 << 20
        ),
        name="local_terms",
    )(
        *hbm(mixed_qkv, mixed_qkv),
        halo,
        halo,
        *hbm(conv_weight, conv_weight, beta, log_decay),
    )


def reader_kernel(
    q_ref,
    qh_ref,
    qw_ref,
    hat_ref,
    decay_ref,
    fresh_ref,
    gate_ref,
    gain_ref,
    own_ref,
    reader_ref,
    scale_ref,
):
    rows = q_ref.shape[0]
    queries = conv_silu(q_ref, qh_ref, qw_ref)
    row_ids, col_ids = square_ids(rows)
    masks = row_ids == col_ids, row_ids >= col_ids, row_ids <= col_ids
    for key in range(READER_KEYS):
        query = key_rows_hat(queries[:, key * DK : (key + 1) * DK]) * DK ** (-0.5)
        raw = three_pass_nt(halves(query), halves(hat_ref[key]))
        for member in range(GROUP):
            head = key * GROUP + member
            cum_col, fading = decay_terms(decay_ref[key, member : member + 1, :], masks)
            mixed = three_pass(fading * raw, fresh_ref[head])
            own_ref[head] = mixed[:, :DV]
            reader_ref[head] = jnp.exp(cum_col) * query - mixed[:, DV:]
            gate = gate_ref[:, head * DV : (head + 1) * DV].astype(f32)
            scale_ref[head] = silu(gate) * gain_ref[...]


def reader_terms(mixed_qkv, halo, conv_weight, log_decay, hats, fresh, out_gate, gain):
    rows = out_gate.shape[0]
    key_cols, step_heads = READER_KEYS * DK, READER_KEYS * GROUP
    value_cols = step_heads * DV
    per_head = pl.BlockSpec((step_heads, rows, DK), lambda i: (i, 0, 0))
    columns = pl.BlockSpec((rows, value_cols), lambda i: (0, i))
    return pl.pallas_call(
        reader_kernel,
        grid=(HK // READER_KEYS,),
        in_specs=[pl.BlockSpec((tall, key_cols), lambda i: (0, i)) for tall in (rows, HALO, CONV)]
        + [
            pl.BlockSpec((READER_KEYS, rows, DK), lambda i: (i, 0, 0)),
            pl.BlockSpec((READER_KEYS, GROUP, rows), lambda i: (i, 0, 0)),
            pl.BlockSpec((step_heads, rows, DV + DK), lambda i: (i, 0, 0)),
            columns,
            pl.BlockSpec((1, DV), lambda i: (0, 0)),
        ],
        out_specs=[per_head, per_head, per_head],
        out_shape=[pltpu.HBM((VALUE_HEAD_SET, rows, DK), f32)] * 3,
        compiler_params=pltpu.CompilerParams(
            dimension_semantics=("arbitrary",), vmem_limit_bytes=24 << 20
        ),
        name="reader_terms",
    )(
        *hbm(mixed_qkv),
        halo,
        *hbm(conv_weight, hats, log_decay, fresh, out_gate),
        gain[None],
    )


def scan_kernel(core_ref, near_ref, far_ref, start_ref, state_ref):
    step, core = pl.program_id(0), core_ref[0]
    block, part_rows = start_ref.shape[:2]

    @pl.when(step == 0)
    def _():
        state_ref[...] = jnp.zeros_like(state_ref)

    is_near = step % 2 == core
    added_at = pl.multiple_of(DK + core * part_rows, 16)
    state = state_ref[...]
    for place in range(block):

        def pick(span):
            return jnp.where(is_near, near_ref[place, span, :], far_ref[place, span, :])

        high, low = halves(state)
        start_ref[place] = high
        transition = pick(slice(0, DK))
        moved = dot(high, transition) + dot(low, transition)
        added = pick(pl.ds(added_at, part_rows)).astype(f32)
        terms = pick(slice(DK + 2 * part_rows, DK + 2 * part_rows + FADE_ROWS)).astype(f32)
        fade = terms[0:1] + (terms[1:2] + terms[2:3])
        state = (fade * state - moved) + added
    state_ref[...] = state


def scan_states(core, near, far, block, part_rows):
    chips, height = near.shape[:2]
    both = pl.BlockSpec((block, height, DK), lambda i, core: (i // 2, 0, 0))
    return pl.pallas_call(
        scan_kernel,
        grid_spec=pltpu.PrefetchScalarGridSpec(
            num_scalar_prefetch=1,
            grid=(2 * chips // block,),
            in_specs=[both, both],
            out_specs=pl.BlockSpec((block, part_rows, DK), lambda i, core: (i, 0, 0)),
            scratch_shapes=[pltpu.VMEM((part_rows, DK), f32)],
        ),
        out_shape=pltpu.HBM((2 * chips, part_rows, DK), bf16),
        compiler_params=pltpu.CompilerParams(
            dimension_semantics=("arbitrary",), vmem_limit_bytes=16 << 20
        ),
        name="scan_states",
    )(core, near, far)


def route_kernel(capacity, routes_ref, gates_ref, select_ref, high_ref, low_ref):
    rows = routes_ref.shape[1]
    experts = select_ref.shape[0] // capacity
    expert_ids = lax.broadcasted_iota(jnp.int32, (experts, rows), 0)
    chosen = jnp.zeros((experts, rows), jnp.bool_)
    gates = jnp.zeros((experts, rows), f32)
    for choice in range(TOPK):
        named = routes_ref[choice : choice + 1, :] == expert_ids
        chosen = chosen | named
        gates = gates + jnp.where(named, gates_ref[choice : choice + 1, :], 0.0)
    row_ids, col_ids = square_ids(rows)
    rank = dot(
        jnp.where(chosen, 1.0, 0.0).astype(bf16),
        jnp.where(row_ids < col_ids, 1.0, 0.0).astype(bf16),
    )
    slot = jnp.where(chosen, rank, -1.0).astype(jnp.int32)
    slot_ids = lax.broadcasted_iota(jnp.int32, (capacity, rows), 0)
    gathers = []
    for expert in range(experts):
        span = slice(expert * capacity, (expert + 1) * capacity)
        taken = slot_ids == slot[expert : expert + 1, :]
        select_ref[span, :] = jnp.where(taken, 1.0, 0.0).astype(bf16)
        gathers.append(jnp.where(taken, gates[expert : expert + 1, :], 0.0))
    high_ref[...], low_ref[...] = halves(jnp.concatenate(gathers, axis=0).T)


def route_tables(routes, route_gates, experts, capacity):
    rows = routes.shape[0]
    slots = experts * capacity
    return pl.pallas_call(
        functools.partial(route_kernel, capacity),
        out_shape=[
            pltpu.HBM((slots, rows), bf16),
            pltpu.HBM((rows, slots), bf16),
            pltpu.HBM((rows, slots), bf16),
        ],
        name="route_tables",
    )(routes.T, route_gates.T)


def mixer_kernel(
    state_ref,
    moe_gain_ref,
    select_hbm,
    own_hbm,
    reader_hbm,
    scale_hbm,
    resid_hbm,
    middle_hbm,
    mixer_hbm,
    rows_hbm,
    select_ref,
    middle_ref,
    own_ref,
    reader_ref,
    scale_ref,
    resid_ref,
    mixer_ref,
    rows_ref,
    in_sems,
    mixer_sems,
    rows_sems,
    middle_sems,
    select_sem,
):
    groups = in_sems.shape[0]
    heads = VALUE_HEAD_SET // groups
    loads, stores = [], []
    for group in range(groups):
        part, columns = pl.ds(group * heads, heads), pl.ds(group * heads * DV, heads * DV)
        loads.append(
            [
                pltpu.make_async_copy(source, target, in_sems.at[group, place])
                for place, (source, target) in enumerate(
                    (
                        (own_hbm.at[part], own_ref.at[part]),
                        (reader_hbm.at[part], reader_ref.at[part]),
                        (scale_hbm.at[part], scale_ref.at[part]),
                        (resid_hbm.at[:, columns], resid_ref.at[:, columns]),
                    )
                )
            ]
        )
        for load in loads[-1]:
            load.start()
    select_load = pltpu.make_async_copy(select_hbm, select_ref, select_sem)
    select_load.start()

    squares = None
    for group in range(groups):
        for load in loads[group]:
            load.wait()
        for head in range(group * heads, (group + 1) * heads):
            span = slice(head * DV, (head + 1) * DV)
            if len(state_ref.shape) == 3:
                state = state_ref[head]
            else:
                block = state_ref.shape[2]
                pieces = [state_ref[head // block, core, head % block] for core in range(2)]
                state = jnp.concatenate(pieces, axis=0)
            high, low = halves(reader_ref[head])
            head_out = own_ref[head] + (dot_nt(high, state) + dot_nt(low, state))
            spread = lax.rsqrt(jnp.mean(head_out * head_out, axis=1, keepdims=True) + 1e-06)
            mixed = (head_out * spread * scale_ref[head]).astype(bf16)
            mixer_ref[:, span] = mixed
            middle = resid_ref[:, span].astype(f32) + mixed.astype(f32)
            middle_ref[head] = middle
            part = jnp.sum(middle * middle, axis=1, keepdims=True)
            squares = part if squares is None else squares + part
        columns = pl.ds(group * heads * DV, heads * DV)
        part = pl.ds(group * heads, heads)
        stores.append(
            pltpu.make_async_copy(middle_ref.at[part], middle_hbm.at[part], middle_sems.at[group])
        )
        stores[-1].start()
        stores.append(
            pltpu.make_async_copy(
                mixer_ref.at[:, columns], mixer_hbm.at[:, columns], mixer_sems.at[group]
            )
        )
        stores[-1].start()

    spread = lax.rsqrt(squares / resid_ref.shape[1] + 1e-06)
    select_load.wait()
    select = select_ref[...]
    for group in range(groups):
        for head in range(group * heads, (group + 1) * heads):
            span = slice(head * DV, (head + 1) * DV)
            moe_input = (middle_ref[head] * spread * moe_gain_ref[:, span]).astype(bf16)
            rows_ref[:, span] = dot(select, moe_input).astype(bf16)
        columns = pl.ds(group * heads * DV, heads * DV)
        stores.append(
            pltpu.make_async_copy(
                rows_ref.at[:, columns], rows_hbm.at[:, columns], rows_sems.at[group]
            )
        )
        stores[-1].start()
    for store in stores:
        store.wait()


def mixer(own, reader, scale, resid, select, state, moe_gain):
    rows, width = resid.shape
    slots, groups = select.shape[0], 4
    local, remote = pl.BlockSpec(memory_space=pltpu.VMEM), pl.BlockSpec(memory_space=pltpu.HBM)
    return pl.pallas_call(
        mixer_kernel,
        in_specs=[local] * 2 + [remote] * 5,
        out_specs=[remote] * 3,
        out_shape=[
            pltpu.HBM((VALUE_HEAD_SET, rows, DV), f32),
            pltpu.HBM((rows, width), bf16),
            pltpu.HBM((slots, width), bf16),
        ],
        scratch_shapes=[pltpu.VMEM((slots, rows), bf16)]
        + [pltpu.VMEM((VALUE_HEAD_SET, rows, DV), f32)] * 4
        + [
            pltpu.VMEM((rows, width), bf16),
            pltpu.VMEM((rows, width), bf16),
            pltpu.VMEM((slots, width), bf16),
            pltpu.SemaphoreType.DMA((groups, 4)),
            pltpu.SemaphoreType.DMA((groups,)),
            pltpu.SemaphoreType.DMA((groups,)),
            pltpu.SemaphoreType.DMA((groups,)),
            pltpu.SemaphoreType.DMA,
        ],
        compiler_params=pltpu.CompilerParams(vmem_limit_bytes=24 << 20),
        name="mixer",
    )(state, moe_gain[None], *hbm(select, own, reader, scale, resid))


def start_loads(sources, buffer_ref, sems):
    loads = [
        pltpu.make_async_copy(source, buffer_ref.at[place], sems.at[place])
        for place, source in enumerate(sources)
    ]
    for load in loads:
        load.start()
    return loads


def expert_in_kernel(order_ref, rows_ref, *refs):
    sources, (result_ref, buffer_ref, sems) = refs[:-3], refs[-3:]
    depth, projected = buffer_ref.shape[1], None
    for place, load in enumerate(start_loads(sources, buffer_ref, sems)):
        start = pl.multiple_of(order_ref[place] * depth, depth)
        load.wait()
        term = dot(rows_ref[:, pl.ds(start, depth)], buffer_ref[place])
        projected = term if projected is None else projected + term
    result_ref[...] = (silu(projected[:, :MOE_H]) * projected[:, MOE_H:]).astype(bf16)


def expert_out_kernel(order_ref, activated_ref, *refs):
    sources, (result_ref, buffer_ref, sems) = refs[:-3], refs[-3:]
    cols, activated = buffer_ref.shape[2], activated_ref[...]
    for place, load in enumerate(start_loads(sources, buffer_ref, sems)):
        start = pl.multiple_of(order_ref[place] * cols, cols)
        load.wait()
        result_ref[:, pl.ds(start, cols)] = dot(activated, buffer_ref[place]).astype(bf16)


def expert_call(kernel, name, order, rows, parts, width):
    local, remote = pl.BlockSpec(memory_space=pltpu.VMEM), pl.BlockSpec(memory_space=pltpu.HBM)
    return pl.pallas_call(
        kernel,
        in_specs=[pl.BlockSpec(memory_space=pltpu.SMEM), local] + [remote] * len(parts),
        out_specs=local,
        out_shape=jax.ShapeDtypeStruct((rows.shape[0], width), bf16),
        scratch_shapes=[
            pltpu.VMEM((len(parts),) + parts[0].shape, bf16),
            pltpu.SemaphoreType.DMA((len(parts),)),
        ],
        compiler_params=pltpu.CompilerParams(vmem_limit_bytes=24 << 20),
        name=name,
    )(order, rows, *hbm(*parts))


def expert_in(order, rows, parts):
    rows = rows.reshape(-1, rows.shape[-1])
    return expert_call(expert_in_kernel, "expert_in", order, rows, parts, MOE_H)


def expert_out(order, activated, parts, width):
    return expert_call(expert_out_kernel, "expert_out", order, activated, parts, width)


def combine_kernel(high_ref, low_ref, middle_ref, rows_ref, out_ref):
    high, low = high_ref[...], low_ref[...]
    for head in range(middle_ref.shape[0]):
        span = slice(head * DV, (head + 1) * DV)
        rows = rows_ref[:, span]
        out_ref[:, span] = (middle_ref[head] + (dot(high, rows) + dot(low, rows))).astype(bf16)


def combine(high, low, middle, rows):
    count, width = middle.shape[1], rows.shape[1]
    return pl.pallas_call(
        combine_kernel,
        out_shape=pltpu.HBM((count, width), bf16),
        compiler_params=pltpu.CompilerParams(vmem_limit_bytes=24 << 20),
        name="combine",
    )(high, low, middle, rows)


def after(value, earlier):
    return lax.optimization_barrier((value, earlier))[0]


def across_halves(value, flip):
    pairs = [
        (core * 2 + half, half * 2 + (core ^ flip)) for core in range(2) for half in range(2)
    ]
    return lax.ppermute(value, ("core", "half"), pairs)


def along_y(value, y_count):
    moved = [value]
    for shift in range(1, y_count):
        pairs = [(source, (source + shift) % y_count) for source in range(y_count)]
        moved.append(lax.ppermute(value, "y", pairs))
    return moved


def shards(
    resid,
    mixed_qkv,
    out_gate,
    beta,
    log_decay,
    conv_weight,
    head_gain,
    moe_gain,
    routes,
    route_gates,
    w_in,
    w_out,
):
    every = ("y", "core", "half", "rest")
    y_count, rest_count = lax.axis_size("y"), lax.axis_size("rest")
    count = lax.axis_size(every)
    experts = 2 * rest_count
    chips, block = count // 2, 2 * rest_count
    splits = chips // VALUE_HEAD_SET
    part = DV // (2 * splits)
    part_rows = round_up(part, 16)
    capacity = round_up(
        max(2, (5 * TOK_DEV * TOPK + 4 * experts - 1) // (4 * experts)), 16
    )
    rows = mixed_qkv.shape[0]
    beta, log_decay = (value.reshape(HK, GROUP, rows) for value in (beta, log_decay))
    tie = lax.optimization_barrier

    halo = lax.ppermute(
        mixed_qkv[rows - HALO :], every, [(source, source + 1) for source in range(count - 1)]
    )
    in_first = across_halves(after(w_in[0], halo), 0)
    send, hats, fresh = local_terms(
        mixed_qkv, halo, conv_weight, beta, log_decay, splits, part, part_rows
    )

    near = lax.all_to_all(
        send.reshape(chips, -1, DK),
        ("y", "half", "rest"),
        split_axis=0,
        concat_axis=0,
        tiled=True,
    )
    hats, in_first = tie((hats, in_first))
    own, reader, scale = reader_terms(
        mixed_qkv, halo, conv_weight, log_decay, hats, fresh, out_gate, head_gain
    )
    select, *gather = route_tables(routes, route_gates, experts, capacity)
    in_first = along_y(in_first, y_count)
    out_first = across_halves(after(w_out[0], send), 0)
    near, in_first, out_first, own, select = tie((near, in_first, out_first, own, select))

    in_second = across_halves(after(w_in[0], near), 1)
    far = lax.ppermute(near, "core", [(0, 1), (1, 0)])
    core = lax.axis_index("core").astype(jnp.int32).reshape(1)
    starts = scan_states(core, near, far, block, part_rows)
    states = lax.all_to_all(starts, every, split_axis=0, concat_axis=0, tiled=True)
    out_first = along_y(out_first, y_count)
    states, in_second, out_first = tie((states, in_second, out_first))

    states = states.reshape(y_count, 2, block, part_rows, DK)
    if part < part_rows or splits > 1:
        states = states[:, :, :, :part].transpose(0, 2, 1, 3, 4)
        states = states.reshape(VALUE_HEAD_SET, DV, DK)
    middle, mixer_out, send_rows = mixer(
        own, reader, scale, resid, select, states, moe_gain
    )
    in_second = along_y(after(in_second, send_rows), y_count)
    out_second = across_halves(after(w_out[0], send_rows), 1)
    out_second = along_y(out_second, y_count)
    exchange = functools.partial(
        lax.all_to_all, axis_name=("core", "rest"), split_axis=0, concat_axis=0, tiled=True
    )
    y_index, half = lax.axis_index("y"), lax.axis_index("half")
    order = jnp.stack(
        [
            (y_index - shift) % y_count * 2 + (half ^ flip)
            for flip in range(2)
            for shift in range(y_count)
        ]
    )
    activated = expert_in(order, exchange(send_rows), in_first + in_second)
    expert_rows = expert_out(order, activated, out_first + out_second, send_rows.shape[1])
    return mixer_out, combine(*gather, middle, exchange(expert_rows))


def solution(mesh):
    ctx_count, ep_count = mesh.shape["ctx"], mesh.shape["ep"]
    names = ("y", "core", "half", "rest")
    fine = Mesh(mesh.devices.reshape(ctx_count // 2, 2, 2, ep_count // 2), names)
    split_rows, split_cols = P(names, None), P(None, names)
    ctx, ep = names[:2], names[2:]
    return jax.shard_map(
        shards,
        mesh=fine,
        in_specs=(
            split_rows,
            split_rows,
            split_rows,
            split_cols,
            split_cols,
            P(),
            P(),
            P(),
            split_rows,
            split_rows,
            P(ep, ctx, None),
            P(ep, None, ctx),
        ),
        out_specs=(split_rows, split_rows),
        check_vma=False,
    )
```

```python
import functools

import jax
import jax.numpy as jnp
from jax import lax
from jax.experimental import pallas as pl
from jax.experimental.pallas import tpu as pltpu
from jax.sharding import Mesh
from jax.sharding import PartitionSpec as P

HK = 8
VALUE_HEAD_SET = 16
DK = 128
DV = 128
MOE_H = 512
CONV = 4
TOPK = 3
TOK_DEV = 128
GROUP = VALUE_HEAD_SET // HK
HALO = 8
STEP_KEYS = 4
READER_KEYS = 2
FADE_ROWS = 16

f32 = jnp.float32
bf16 = jnp.bfloat16


def round_up(value, multiple):
    return (value + multiple - 1) // multiple * multiple


def hbm(*arrays):
    return [pltpu.with_memory_space_constraint(array, pltpu.HBM) for array in arrays]


def dot(lhs, rhs):
    return jnp.dot(lhs, rhs, preferred_element_type=f32)


def dot_nt(lhs, rhs):
    return lax.dot_general(lhs, rhs, (((1,), (1,)), ((), ())), preferred_element_type=f32)


def halves(value):
    high = value.astype(bf16)
    return high, (value - high.astype(f32)).astype(bf16)


def one_pass(lhs, rhs):
    return dot(lhs.astype(bf16), rhs.astype(bf16))


def three_pass(lhs, rhs):
    (lhs_high, lhs_low), (rhs_high, rhs_low) = halves(lhs), halves(rhs)
    return dot(lhs_high, rhs_high) + (dot(lhs_high, rhs_low) + dot(lhs_low, rhs_high))


def three_pass_nt(lhs, rhs):
    (lhs_high, lhs_low), (rhs_high, rhs_low) = lhs, rhs
    return dot_nt(lhs_high, rhs_high) + (dot_nt(lhs_high, rhs_low) + dot_nt(lhs_low, rhs_high))


def silu(value):
    return value * jax.nn.sigmoid(value)


def conv_silu(ref, halo_ref, weight_ref):
    rows = ref.shape[0]
    padded = jnp.concatenate([halo_ref[...].astype(f32), ref[...].astype(f32)], axis=0)
    total = padded[HALO:] * weight_ref[CONV - 1 : CONV, :]
    for tap in range(CONV - 1):
        start = HALO - (CONV - 1) + tap
        total = total + padded[start : start + rows] * weight_ref[tap : tap + 1, :]
    return silu(total)


def fade_tile(fade):
    left = jnp.broadcast_to(fade, (FADE_ROWS, DK))
    row_ids = lax.broadcasted_iota(jnp.int32, (FADE_ROWS, DK), 0)
    tile = jnp.zeros((FADE_ROWS, DK), f32)
    for term in range(3):
        part = left.astype(bf16).astype(f32)
        tile = jnp.where(row_ids == term, part, tile)
        left = left - part
    return tile.astype(bf16)


def key_rows_hat(key_rows):
    return key_rows * lax.rsqrt(jnp.sum(key_rows * key_rows, axis=1, keepdims=True) + 1e-06)


def decay_terms(decay_row, masks):
    diagonal, causal, upper = masks
    decay_col = jnp.sum(jnp.where(diagonal, decay_row, 0.0), axis=1, keepdims=True)
    cum_col = jnp.sum(jnp.where(causal, decay_row, 0.0), axis=1, keepdims=True)
    cum_row = jnp.sum(jnp.where(upper, decay_col, 0.0), axis=0, keepdims=True)
    fading = jnp.where(causal, jnp.exp(jnp.where(causal, cum_col - cum_row, 0.0)), 0.0)
    return cum_col, fading


def square_ids(rows):
    return (
        lax.broadcasted_iota(jnp.int32, (rows, rows), 0),
        lax.broadcasted_iota(jnp.int32, (rows, rows), 1),
    )


def local_kernel(
    splits,
    part,
    part_rows,
    k_ref,
    v_ref,
    kh_ref,
    vh_ref,
    kw_ref,
    vw_ref,
    beta_ref,
    decay_ref,
    send_ref,
    hat_ref,
    fresh_ref,
):
    rows = k_ref.shape[0]
    keys, values = conv_silu(k_ref, kh_ref, kw_ref), conv_silu(v_ref, vh_ref, vw_ref)
    row_ids, col_ids = square_ids(rows)
    strict, causal, diagonal = row_ids > col_ids, row_ids >= col_ids, row_ids == col_ids
    masks = diagonal, causal, row_ids <= col_ids
    identity = jnp.where(diagonal, 1.0, 0.0).astype(f32)

    key_hats, grams = [], []
    for key in range(STEP_KEYS):
        key_hat = key_rows_hat(keys[:, key * DK : (key + 1) * DK])
        hat_ref[key] = key_hat
        key_hats.append(key_hat)
        parts = halves(key_hat)
        grams.append(three_pass_nt(parts, parts))

    heads = range(STEP_KEYS * GROUP)
    lower, betas, fades, tails, wholes = [], [], [], [], []
    for head in heads:
        key, member = head // GROUP, head % GROUP
        beta_row = beta_ref[key, member : member + 1, :]
        decay_row = decay_ref[key, member : member + 1, :]
        beta_col = jnp.sum(jnp.where(diagonal, beta_row, 0.0), axis=1, keepdims=True)
        cum_col, fading = decay_terms(decay_row, masks)
        last = jnp.sum(decay_row, axis=1, keepdims=True)
        lower.append(jnp.where(strict, beta_col * fading * grams[key], 0.0))
        betas.append(beta_col)
        fades.append(jnp.exp(cum_col))
        tails.append(jnp.exp(jnp.minimum(last - cum_col, 0.0)))
        wholes.append(jnp.exp(last))

    solved = [
        jnp.where(row_ids // 2 == col_ids // 2, identity - lower[head], 0.0) for head in heads
    ]
    size = 2
    while size < rows:
        joins = (row_ids // (2 * size) == col_ids // (2 * size)) & (
            row_ids // size != col_ids // size
        )
        parts = [solved[head].astype(bf16) for head in heads]
        inner = [
            dot(parts[head], jnp.where(joins, lower[head], 0.0).astype(bf16)) for head in heads
        ]
        solved = [solved[head] - dot(inner[head].astype(bf16), parts[head]) for head in heads]
        size *= 2
    residues = [
        (identity - solved[head]) - three_pass(lower[head], solved[head]) for head in heads
    ]
    solved = [solved[head] + one_pass(solved[head], residues[head]) for head in heads]

    for head in heads:
        key = head // GROUP
        value_span = slice(head * DV, (head + 1) * DV)
        fresh_carried = three_pass(
            solved[head],
            jnp.concatenate(
                [
                    betas[head] * values[:, value_span],
                    (betas[head] * fades[head]) * key_hats[key],
                ],
                axis=1,
            ),
        )
        fresh_ref[head] = fresh_carried
        sums = three_pass(fresh_carried.T, tails[head] * key_hats[key])
        transition, state_add = sums[DV:].astype(bf16), sums[:DV].astype(bf16)
        fade_rows = fade_tile(wholes[head])
        for split in range(splits):
            send_ref[head, split, :DK, :] = transition
            for core in range(2):
                place = 2 * split + core
                added = state_add[place * part : (place + 1) * part]
                if part < part_rows:
                    added = jnp.concatenate(
                        [added, jnp.zeros((part_rows - part, DK), bf16)], axis=0
                    )
                send_ref[head, split, pl.ds(DK + core * part_rows, part_rows), :] = added
            send_ref[head, split, pl.ds(DK + 2 * part_rows, FADE_ROWS), :] = fade_rows


def local_terms(mixed_qkv, halo, conv_weight, beta, log_decay, splits, part, part_rows):
    rows = mixed_qkv.shape[0]
    key_cols, value_cols = STEP_KEYS * DK, STEP_KEYS * GROUP * DV
    steps = HK // STEP_KEYS
    value_from = 2 * HK * DK // value_cols
    height = DK + 2 * part_rows + FADE_ROWS
    col_maps = (
        (key_cols, lambda i: (0, steps + i)),
        (value_cols, lambda i: (0, value_from + i)),
    )
    specs = [
        pl.BlockSpec((tall, width), index)
        for tall in (rows, HALO, CONV)
        for width, index in col_maps
    ]
    per_key = pl.BlockSpec((STEP_KEYS, GROUP, rows), lambda i: (i, 0, 0))
    step_heads = STEP_KEYS * GROUP
    return pl.pallas_call(
        functools.partial(local_kernel, splits, part, part_rows),
        grid=(steps,),
        in_specs=specs + [per_key, per_key],
        out_specs=[
            pl.BlockSpec((step_heads, splits, height, DK), lambda i: (i, 0, 0, 0)),
            pl.BlockSpec((STEP_KEYS, rows, DK), lambda i: (i, 0, 0)),
            pl.BlockSpec((step_heads, rows, DV + DK), lambda i: (i, 0, 0)),
        ],
        out_shape=[
            pltpu.HBM((VALUE_HEAD_SET, splits, height, DK), bf16),
            pltpu.HBM((HK, rows, DK), f32),
            pltpu.HBM((VALUE_HEAD_SET, rows, DV + DK), f32),
        ],
        compiler_params=pltpu.CompilerParams(
            dimension_semantics=("arbitrary",), vmem_limit_bytes=24 << 20
        ),
        name="local_terms",
    )(
        *hbm(mixed_qkv, mixed_qkv),
        halo,
        halo,
        *hbm(conv_weight, conv_weight, beta, log_decay),
    )


def reader_kernel(
    q_ref,
    qh_ref,
    qw_ref,
    hat_ref,
    decay_ref,
    fresh_ref,
    gate_ref,
    gain_ref,
    own_ref,
    reader_ref,
    scale_ref,
):
    rows = q_ref.shape[0]
    queries = conv_silu(q_ref, qh_ref, qw_ref)
    row_ids, col_ids = square_ids(rows)
    masks = row_ids == col_ids, row_ids >= col_ids, row_ids <= col_ids
    for key in range(READER_KEYS):
        query = key_rows_hat(queries[:, key * DK : (key + 1) * DK]) * DK ** (-0.5)
        raw = three_pass_nt(halves(query), halves(hat_ref[key]))
        for member in range(GROUP):
            head = key * GROUP + member
            cum_col, fading = decay_terms(decay_ref[key, member : member + 1, :], masks)
            mixed = three_pass(fading * raw, fresh_ref[head])
            own_ref[head] = mixed[:, :DV]
            reader_ref[head] = jnp.exp(cum_col) * query - mixed[:, DV:]
            gate = gate_ref[:, head * DV : (head + 1) * DV].astype(f32)
            scale_ref[head] = silu(gate) * gain_ref[...]


def reader_terms(mixed_qkv, halo, conv_weight, log_decay, hats, fresh, out_gate, gain):
    rows = out_gate.shape[0]
    key_cols, step_heads = READER_KEYS * DK, READER_KEYS * GROUP
    value_cols = step_heads * DV
    per_head = pl.BlockSpec((step_heads, rows, DK), lambda i: (i, 0, 0))
    columns = pl.BlockSpec((rows, value_cols), lambda i: (0, i))
    return pl.pallas_call(
        reader_kernel,
        grid=(HK // READER_KEYS,),
        in_specs=[pl.BlockSpec((tall, key_cols), lambda i: (0, i)) for tall in (rows, HALO, CONV)]
        + [
            pl.BlockSpec((READER_KEYS, rows, DK), lambda i: (i, 0, 0)),
            pl.BlockSpec((READER_KEYS, GROUP, rows), lambda i: (i, 0, 0)),
            pl.BlockSpec((step_heads, rows, DV + DK), lambda i: (i, 0, 0)),
            columns,
            pl.BlockSpec((1, DV), lambda i: (0, 0)),
        ],
        out_specs=[per_head, per_head, per_head],
        out_shape=[pltpu.HBM((VALUE_HEAD_SET, rows, DK), f32)] * 3,
        compiler_params=pltpu.CompilerParams(
            dimension_semantics=("arbitrary",), vmem_limit_bytes=24 << 20
        ),
        name="reader_terms",
    )(
        *hbm(mixed_qkv),
        halo,
        *hbm(conv_weight, hats, log_decay, fresh, out_gate),
        gain[None],
    )


def scan_kernel(core_ref, near_ref, far_ref, start_ref, state_ref):
    step, core = pl.program_id(0), core_ref[0]
    block, part_rows = start_ref.shape[:2]

    @pl.when(step == 0)
    def _():
        state_ref[...] = jnp.zeros_like(state_ref)

    is_near = step % 2 == core
    added_at = pl.multiple_of(DK + core * part_rows, 16)
    state = state_ref[...]
    for place in range(block):

        def pick(span):
            return jnp.where(is_near, near_ref[place, span, :], far_ref[place, span, :])

        high, low = halves(state)
        start_ref[place] = high
        transition = pick(slice(0, DK))
        moved = dot(high, transition) + dot(low, transition)
        added = pick(pl.ds(added_at, part_rows)).astype(f32)
        terms = pick(slice(DK + 2 * part_rows, DK + 2 * part_rows + FADE_ROWS)).astype(f32)
        fade = terms[0:1] + (terms[1:2] + terms[2:3])
        state = (fade * state - moved) + added
    state_ref[...] = state


def scan_states(core, near, far, block, part_rows):
    chips, height = near.shape[:2]
    both = pl.BlockSpec((block, height, DK), lambda i, core: (i // 2, 0, 0))
    return pl.pallas_call(
        scan_kernel,
        grid_spec=pltpu.PrefetchScalarGridSpec(
            num_scalar_prefetch=1,
            grid=(2 * chips // block,),
            in_specs=[both, both],
            out_specs=pl.BlockSpec((block, part_rows, DK), lambda i, core: (i, 0, 0)),
            scratch_shapes=[pltpu.VMEM((part_rows, DK), f32)],
        ),
        out_shape=pltpu.HBM((2 * chips, part_rows, DK), bf16),
        compiler_params=pltpu.CompilerParams(
            dimension_semantics=("arbitrary",), vmem_limit_bytes=16 << 20
        ),
        name="scan_states",
    )(core, near, far)


def route_kernel(capacity, routes_ref, gates_ref, select_ref, high_ref, low_ref):
    rows = routes_ref.shape[1]
    experts = select_ref.shape[0] // capacity
    expert_ids = lax.broadcasted_iota(jnp.int32, (experts, rows), 0)
    chosen = jnp.zeros((experts, rows), jnp.bool_)
    gates = jnp.zeros((experts, rows), f32)
    for choice in range(TOPK):
        named = routes_ref[choice : choice + 1, :] == expert_ids
        chosen = chosen | named
        gates = gates + jnp.where(named, gates_ref[choice : choice + 1, :], 0.0)
    row_ids, col_ids = square_ids(rows)
    rank = dot(
        jnp.where(chosen, 1.0, 0.0).astype(bf16),
        jnp.where(row_ids < col_ids, 1.0, 0.0).astype(bf16),
    )
    slot = jnp.where(chosen, rank, -1.0).astype(jnp.int32)
    slot_ids = lax.broadcasted_iota(jnp.int32, (capacity, rows), 0)
    gathers = []
    for expert in range(experts):
        span = slice(expert * capacity, (expert + 1) * capacity)
        taken = slot_ids == slot[expert : expert + 1, :]
        select_ref[span, :] = jnp.where(taken, 1.0, 0.0).astype(bf16)
        gathers.append(jnp.where(taken, gates[expert : expert + 1, :], 0.0))
    high_ref[...], low_ref[...] = halves(jnp.concatenate(gathers, axis=0).T)


def route_tables(routes, route_gates, experts, capacity):
    rows = routes.shape[0]
    slots = experts * capacity
    return pl.pallas_call(
        functools.partial(route_kernel, capacity),
        out_shape=[
            pltpu.HBM((slots, rows), bf16),
            pltpu.HBM((rows, slots), bf16),
            pltpu.HBM((rows, slots), bf16),
        ],
        name="route_tables",
    )(routes.T, route_gates.T)


def mixer_kernel(
    state_ref,
    moe_gain_ref,
    select_hbm,
    own_hbm,
    reader_hbm,
    scale_hbm,
    resid_hbm,
    middle_hbm,
    mixer_hbm,
    rows_hbm,
    select_ref,
    middle_ref,
    own_ref,
    reader_ref,
    scale_ref,
    resid_ref,
    mixer_ref,
    rows_ref,
    in_sems,
    mixer_sems,
    rows_sems,
    middle_sems,
    select_sem,
):
    groups = in_sems.shape[0]
    heads = VALUE_HEAD_SET // groups
    loads, stores = [], []
    for group in range(groups):
        part, columns = pl.ds(group * heads, heads), pl.ds(group * heads * DV, heads * DV)
        loads.append(
            [
                pltpu.make_async_copy(source, target, in_sems.at[group, place])
                for place, (source, target) in enumerate(
                    (
                        (own_hbm.at[part], own_ref.at[part]),
                        (reader_hbm.at[part], reader_ref.at[part]),
                        (scale_hbm.at[part], scale_ref.at[part]),
                        (resid_hbm.at[:, columns], resid_ref.at[:, columns]),
                    )
                )
            ]
        )
        for load in loads[-1]:
            load.start()
    select_load = pltpu.make_async_copy(select_hbm, select_ref, select_sem)
    select_load.start()

    squares = None
    for group in range(groups):
        for load in loads[group]:
            load.wait()
        for head in range(group * heads, (group + 1) * heads):
            span = slice(head * DV, (head + 1) * DV)
            if len(state_ref.shape) == 3:
                state = state_ref[head]
            else:
                block = state_ref.shape[2]
                pieces = [state_ref[head // block, core, head % block] for core in range(2)]
                state = jnp.concatenate(pieces, axis=0)
            high, low = halves(reader_ref[head])
            head_out = own_ref[head] + (dot_nt(high, state) + dot_nt(low, state))
            spread = lax.rsqrt(jnp.mean(head_out * head_out, axis=1, keepdims=True) + 1e-06)
            mixed = (head_out * spread * scale_ref[head]).astype(bf16)
            mixer_ref[:, span] = mixed
            middle = resid_ref[:, span].astype(f32) + mixed.astype(f32)
            middle_ref[head] = middle
            part = jnp.sum(middle * middle, axis=1, keepdims=True)
            squares = part if squares is None else squares + part
        columns = pl.ds(group * heads * DV, heads * DV)
        part = pl.ds(group * heads, heads)
        stores.append(
            pltpu.make_async_copy(middle_ref.at[part], middle_hbm.at[part], middle_sems.at[group])
        )
        stores[-1].start()
        stores.append(
            pltpu.make_async_copy(
                mixer_ref.at[:, columns], mixer_hbm.at[:, columns], mixer_sems.at[group]
            )
        )
        stores[-1].start()

    spread = lax.rsqrt(squares / resid_ref.shape[1] + 1e-06)
    select_load.wait()
    select = select_ref[...]
    for group in range(groups):
        for head in range(group * heads, (group + 1) * heads):
            span = slice(head * DV, (head + 1) * DV)
            moe_input = (middle_ref[head] * spread * moe_gain_ref[:, span]).astype(bf16)
            rows_ref[:, span] = dot(select, moe_input).astype(bf16)
        columns = pl.ds(group * heads * DV, heads * DV)
        stores.append(
            pltpu.make_async_copy(
                rows_ref.at[:, columns], rows_hbm.at[:, columns], rows_sems.at[group]
            )
        )
        stores[-1].start()
    for store in stores:
        store.wait()


def mixer(own, reader, scale, resid, select, state, moe_gain):
    rows, width = resid.shape
    slots, groups = select.shape[0], 4
    local, remote = pl.BlockSpec(memory_space=pltpu.VMEM), pl.BlockSpec(memory_space=pltpu.HBM)
    return pl.pallas_call(
        mixer_kernel,
        in_specs=[local] * 2 + [remote] * 5,
        out_specs=[remote] * 3,
        out_shape=[
            pltpu.HBM((VALUE_HEAD_SET, rows, DV), f32),
            pltpu.HBM((rows, width), bf16),
            pltpu.HBM((slots, width), bf16),
        ],
        scratch_shapes=[pltpu.VMEM((slots, rows), bf16)]
        + [pltpu.VMEM((VALUE_HEAD_SET, rows, DV), f32)] * 4
        + [
            pltpu.VMEM((rows, width), bf16),
            pltpu.VMEM((rows, width), bf16),
            pltpu.VMEM((slots, width), bf16),
            pltpu.SemaphoreType.DMA((groups, 4)),
            pltpu.SemaphoreType.DMA((groups,)),
            pltpu.SemaphoreType.DMA((groups,)),
            pltpu.SemaphoreType.DMA((groups,)),
            pltpu.SemaphoreType.DMA,
        ],
        compiler_params=pltpu.CompilerParams(vmem_limit_bytes=24 << 20),
        name="mixer",
    )(state, moe_gain[None], *hbm(select, own, reader, scale, resid))


def start_loads(sources, buffer_ref, sems):
    loads = [
        pltpu.make_async_copy(source, buffer_ref.at[place], sems.at[place])
        for place, source in enumerate(sources)
    ]
    for load in loads:
        load.start()
    return loads


def expert_in_kernel(order_ref, rows_ref, *refs):
    sources, (result_ref, buffer_ref, sems) = refs[:-3], refs[-3:]
    depth, projected = buffer_ref.shape[1], None
    for place, load in enumerate(start_loads(sources, buffer_ref, sems)):
        start = pl.multiple_of(order_ref[place] * depth, depth)
        load.wait()
        term = dot(rows_ref[:, pl.ds(start, depth)], buffer_ref[place])
        projected = term if projected is None else projected + term
    result_ref[...] = (silu(projected[:, :MOE_H]) * projected[:, MOE_H:]).astype(bf16)


def expert_out_kernel(order_ref, activated_ref, *refs):
    sources, (result_ref, buffer_ref, sems) = refs[:-3], refs[-3:]
    cols, activated = buffer_ref.shape[2], activated_ref[...]
    for place, load in enumerate(start_loads(sources, buffer_ref, sems)):
        start = pl.multiple_of(order_ref[place] * cols, cols)
        load.wait()
        result_ref[:, pl.ds(start, cols)] = dot(activated, buffer_ref[place]).astype(bf16)


def expert_call(kernel, name, order, rows, parts, width):
    local, remote = pl.BlockSpec(memory_space=pltpu.VMEM), pl.BlockSpec(memory_space=pltpu.HBM)
    return pl.pallas_call(
        kernel,
        in_specs=[pl.BlockSpec(memory_space=pltpu.SMEM), local] + [remote] * len(parts),
        out_specs=local,
        out_shape=jax.ShapeDtypeStruct((rows.shape[0], width), bf16),
        scratch_shapes=[
            pltpu.VMEM((len(parts),) + parts[0].shape, bf16),
            pltpu.SemaphoreType.DMA((len(parts),)),
        ],
        compiler_params=pltpu.CompilerParams(vmem_limit_bytes=24 << 20),
        name=name,
    )(order, rows, *hbm(*parts))


def expert_in(order, rows, parts):
    rows = rows.reshape(-1, rows.shape[-1])
    return expert_call(expert_in_kernel, "expert_in", order, rows, parts, MOE_H)


def expert_out(order, activated, parts, width):
    return expert_call(expert_out_kernel, "expert_out", order, activated, parts, width)


def combine_kernel(high_ref, low_ref, middle_ref, rows_ref, out_ref):
    high, low = high_ref[...], low_ref[...]
    for head in range(middle_ref.shape[0]):
        span = slice(head * DV, (head + 1) * DV)
        rows = rows_ref[:, span]
        out_ref[:, span] = (middle_ref[head] + (dot(high, rows) + dot(low, rows))).astype(bf16)


def combine(high, low, middle, rows):
    count, width = middle.shape[1], rows.shape[1]
    return pl.pallas_call(
        combine_kernel,
        out_shape=pltpu.HBM((count, width), bf16),
        compiler_params=pltpu.CompilerParams(vmem_limit_bytes=24 << 20),
        name="combine",
    )(high, low, middle, rows)


def after(value, earlier):
    return lax.optimization_barrier((value, earlier))[0]


def across_halves(value, flip):
    pairs = [
        (core * 2 + half, half * 2 + (core ^ flip)) for core in range(2) for half in range(2)
    ]
    return lax.ppermute(value, ("core", "half"), pairs)


def along_y(value, y_count):
    moved = [value]
    for shift in range(1, y_count):
        pairs = [(source, (source + shift) % y_count) for source in range(y_count)]
        moved.append(lax.ppermute(value, "y", pairs))
    return moved


def shards(
    resid,
    mixed_qkv,
    out_gate,
    beta,
    log_decay,
    conv_weight,
    head_gain,
    moe_gain,
    routes,
    route_gates,
    w_in,
    w_out,
):
    every = ("y", "core", "half", "rest")
    y_count, rest_count = lax.axis_size("y"), lax.axis_size("rest")
    count = lax.axis_size(every)
    experts = 2 * rest_count
    chips, block = count // 2, 2 * rest_count
    splits = chips // VALUE_HEAD_SET
    part = DV // (2 * splits)
    part_rows = round_up(part, 16)
    capacity = round_up(
        max(2, (5 * TOK_DEV * TOPK + 4 * experts - 1) // (4 * experts)), 16
    )
    rows = mixed_qkv.shape[0]
    beta, log_decay = (value.reshape(HK, GROUP, rows) for value in (beta, log_decay))
    tie = lax.optimization_barrier

    rim = mixed_qkv[rows - HALO :]
    halo = lax.ppermute(rim, every, [(source, source + 1) for source in range(count - 1)])
    in_first = across_halves(after(w_in[0], rim), 0)
    send, hats, fresh = local_terms(
        mixed_qkv, halo, conv_weight, beta, log_decay, splits, part, part_rows
    )

    near = lax.all_to_all(
        send.reshape(chips, -1, DK),
        ("y", "half", "rest"),
        split_axis=0,
        concat_axis=0,
        tiled=True,
    )
    hats, in_first = tie((hats, in_first))
    own, reader, scale = reader_terms(
        mixed_qkv, halo, conv_weight, log_decay, hats, fresh, out_gate, head_gain
    )
    select, *gather = route_tables(routes, route_gates, experts, capacity)
    in_first = along_y(in_first, y_count)
    out_first = across_halves(after(w_out[0], send), 0)
    near, in_first, out_first, own, select = tie((near, in_first, out_first, own, select))

    in_second = across_halves(after(w_in[0], near), 1)
    far = lax.ppermute(near, "core", [(0, 1), (1, 0)])
    core = lax.axis_index("core").astype(jnp.int32).reshape(1)
    starts = scan_states(core, near, far, block, part_rows)
    states = lax.all_to_all(starts, every, split_axis=0, concat_axis=0, tiled=True)
    out_first = along_y(out_first, y_count)
    states, in_second, out_first = tie((states, in_second, out_first))

    states = states.reshape(y_count, 2, block, part_rows, DK)
    if part < part_rows or splits > 1:
        states = states[:, :, :, :part].transpose(0, 2, 1, 3, 4)
        states = states.reshape(VALUE_HEAD_SET, DV, DK)
    middle, mixer_out, send_rows = mixer(
        own, reader, scale, resid, select, states, moe_gain
    )
    in_second = along_y(after(in_second, send_rows), y_count)
    out_second = across_halves(after(w_out[0], send_rows), 1)
    out_second = along_y(out_second, y_count)
    exchange = functools.partial(
        lax.all_to_all, axis_name=("core", "rest"), split_axis=0, concat_axis=0, tiled=True
    )
    y_index, half = lax.axis_index("y"), lax.axis_index("half")
    order = jnp.stack(
        [
            (y_index - shift) % y_count * 2 + (half ^ flip)
            for flip in range(2)
            for shift in range(y_count)
        ]
    )
    activated = expert_in(order, exchange(send_rows), in_first + in_second)
    expert_rows = expert_out(order, activated, out_first + out_second, send_rows.shape[1])
    return mixer_out, combine(*gather, middle, exchange(expert_rows))


def solution(mesh):
    ctx_count, ep_count = mesh.shape["ctx"], mesh.shape["ep"]
    names = ("y", "core", "half", "rest")
    fine = Mesh(mesh.devices.reshape(ctx_count // 2, 2, 2, ep_count // 2), names)
    split_rows, split_cols = P(names, None), P(None, names)
    ctx, ep = names[:2], names[2:]
    return jax.shard_map(
        shards,
        mesh=fine,
        in_specs=(
            split_rows,
            split_rows,
            split_rows,
            split_cols,
            split_cols,
            P(),
            P(),
            P(),
            split_rows,
            split_rows,
            P(ep, ctx, None),
            P(ep, None, ctx),
        ),
        out_specs=(split_rows, split_rows),
        check_vma=False,
    )
```

```python
import functools

import jax
import jax.numpy as jnp
from jax import lax
from jax.experimental import pallas as pl
from jax.experimental.pallas import tpu as pltpu
from jax.sharding import Mesh
from jax.sharding import PartitionSpec as P

HK = 8
VALUE_HEAD_SET = 16
DK = 128
DV = 128
MOE_H = 512
CONV = 4
TOPK = 3
TOK_DEV = 128
GROUP = VALUE_HEAD_SET // HK
HALO = 8
STEP_KEYS = 4
READER_KEYS = 4
FADE_ROWS = 16

f32 = jnp.float32
bf16 = jnp.bfloat16


def round_up(value, multiple):
    return (value + multiple - 1) // multiple * multiple


def hbm(*arrays):
    return [pltpu.with_memory_space_constraint(array, pltpu.HBM) for array in arrays]


def dot(lhs, rhs):
    return jnp.dot(lhs, rhs, preferred_element_type=f32)


def dot_nt(lhs, rhs):
    return lax.dot_general(lhs, rhs, (((1,), (1,)), ((), ())), preferred_element_type=f32)


def halves(value):
    high = value.astype(bf16)
    return high, (value - high.astype(f32)).astype(bf16)


def one_pass(lhs, rhs):
    return dot(lhs.astype(bf16), rhs.astype(bf16))


def three_pass(lhs, rhs):
    (lhs_high, lhs_low), (rhs_high, rhs_low) = halves(lhs), halves(rhs)
    return dot(lhs_high, rhs_high) + (dot(lhs_high, rhs_low) + dot(lhs_low, rhs_high))


def three_pass_nt(lhs, rhs):
    (lhs_high, lhs_low), (rhs_high, rhs_low) = lhs, rhs
    return dot_nt(lhs_high, rhs_high) + (dot_nt(lhs_high, rhs_low) + dot_nt(lhs_low, rhs_high))


def silu(value):
    return value * jax.nn.sigmoid(value)


def conv_silu(ref, halo_ref, weight_ref):
    rows = ref.shape[0]
    padded = jnp.concatenate([halo_ref[...].astype(f32), ref[...].astype(f32)], axis=0)
    total = padded[HALO:] * weight_ref[CONV - 1 : CONV, :]
    for tap in range(CONV - 1):
        start = HALO - (CONV - 1) + tap
        total = total + padded[start : start + rows] * weight_ref[tap : tap + 1, :]
    return silu(total)


def fade_tile(fade):
    left = jnp.broadcast_to(fade, (FADE_ROWS, DK))
    row_ids = lax.broadcasted_iota(jnp.int32, (FADE_ROWS, DK), 0)
    tile = jnp.zeros((FADE_ROWS, DK), f32)
    for term in range(3):
        part = left.astype(bf16).astype(f32)
        tile = jnp.where(row_ids == term, part, tile)
        left = left - part
    return tile.astype(bf16)


def key_rows_hat(key_rows):
    return key_rows * lax.rsqrt(jnp.sum(key_rows * key_rows, axis=1, keepdims=True) + 1e-06)


def decay_terms(decay_row, masks):
    diagonal, causal, upper = masks
    decay_col = jnp.sum(jnp.where(diagonal, decay_row, 0.0), axis=1, keepdims=True)
    cum_col = jnp.sum(jnp.where(causal, decay_row, 0.0), axis=1, keepdims=True)
    cum_row = jnp.sum(jnp.where(upper, decay_col, 0.0), axis=0, keepdims=True)
    fading = jnp.where(causal, jnp.exp(jnp.where(causal, cum_col - cum_row, 0.0)), 0.0)
    return cum_col, fading


def square_ids(rows):
    return (
        lax.broadcasted_iota(jnp.int32, (rows, rows), 0),
        lax.broadcasted_iota(jnp.int32, (rows, rows), 1),
    )


def local_kernel(
    splits,
    part,
    part_rows,
    k_ref,
    v_ref,
    kh_ref,
    vh_ref,
    kw_ref,
    vw_ref,
    beta_ref,
    decay_ref,
    send_ref,
    hat_ref,
    fresh_ref,
):
    rows = k_ref.shape[0]
    keys, values = conv_silu(k_ref, kh_ref, kw_ref), conv_silu(v_ref, vh_ref, vw_ref)
    row_ids, col_ids = square_ids(rows)
    strict, causal, diagonal = row_ids > col_ids, row_ids >= col_ids, row_ids == col_ids
    masks = diagonal, causal, row_ids <= col_ids
    identity = jnp.where(diagonal, 1.0, 0.0).astype(f32)

    key_hats, grams = [], []
    for key in range(STEP_KEYS):
        key_hat = key_rows_hat(keys[:, key * DK : (key + 1) * DK])
        hat_ref[key] = key_hat
        key_hats.append(key_hat)
        parts = halves(key_hat)
        grams.append(three_pass_nt(parts, parts))

    heads = range(STEP_KEYS * GROUP)
    lower, betas, fades, tails, wholes = [], [], [], [], []
    for head in heads:
        key, member = head // GROUP, head % GROUP
        beta_row = beta_ref[key, member : member + 1, :]
        decay_row = decay_ref[key, member : member + 1, :]
        beta_col = jnp.sum(jnp.where(diagonal, beta_row, 0.0), axis=1, keepdims=True)
        cum_col, fading = decay_terms(decay_row, masks)
        last = jnp.sum(decay_row, axis=1, keepdims=True)
        lower.append(jnp.where(strict, beta_col * fading * grams[key], 0.0))
        betas.append(beta_col)
        fades.append(jnp.exp(cum_col))
        tails.append(jnp.exp(jnp.minimum(last - cum_col, 0.0)))
        wholes.append(jnp.exp(last))

    solved = [
        jnp.where(row_ids // 2 == col_ids // 2, identity - lower[head], 0.0) for head in heads
    ]
    size = 2
    while size < rows:
        joins = (row_ids // (2 * size) == col_ids // (2 * size)) & (
            row_ids // size != col_ids // size
        )
        parts = [solved[head].astype(bf16) for head in heads]
        inner = [
            dot(parts[head], jnp.where(joins, lower[head], 0.0).astype(bf16)) for head in heads
        ]
        solved = [solved[head] - dot(inner[head].astype(bf16), parts[head]) for head in heads]
        size *= 2
    residues = [
        (identity - solved[head]) - three_pass(lower[head], solved[head]) for head in heads
    ]
    solved = [solved[head] + one_pass(solved[head], residues[head]) for head in heads]

    for head in heads:
        key = head // GROUP
        value_span = slice(head * DV, (head + 1) * DV)
        fresh_carried = three_pass(
            solved[head],
            jnp.concatenate(
                [
                    betas[head] * values[:, value_span],
                    (betas[head] * fades[head]) * key_hats[key],
                ],
                axis=1,
            ),
        )
        fresh_ref[head] = fresh_carried
        sums = three_pass(fresh_carried.T, tails[head] * key_hats[key])
        transition, state_add = sums[DV:].astype(bf16), sums[:DV].astype(bf16)
        fade_rows = fade_tile(wholes[head])
        for split in range(splits):
            send_ref[head, split, :DK, :] = transition
            for core in range(2):
                place = 2 * split + core
                added = state_add[place * part : (place + 1) * part]
                if part < part_rows:
                    added = jnp.concatenate(
                        [added, jnp.zeros((part_rows - part, DK), bf16)], axis=0
                    )
                send_ref[head, split, pl.ds(DK + core * part_rows, part_rows), :] = added
            send_ref[head, split, pl.ds(DK + 2 * part_rows, FADE_ROWS), :] = fade_rows


def local_terms(mixed_qkv, halo, conv_weight, beta, log_decay, splits, part, part_rows):
    rows = mixed_qkv.shape[0]
    key_cols, value_cols = STEP_KEYS * DK, STEP_KEYS * GROUP * DV
    steps = HK // STEP_KEYS
    value_from = 2 * HK * DK // value_cols
    height = DK + 2 * part_rows + FADE_ROWS
    col_maps = (
        (key_cols, lambda i: (0, steps + i)),
        (value_cols, lambda i: (0, value_from + i)),
    )
    specs = [
        pl.BlockSpec((tall, width), index)
        for tall in (rows, HALO, CONV)
        for width, index in col_maps
    ]
    per_key = pl.BlockSpec((STEP_KEYS, GROUP, rows), lambda i: (i, 0, 0))
    step_heads = STEP_KEYS * GROUP
    return pl.pallas_call(
        functools.partial(local_kernel, splits, part, part_rows),
        grid=(steps,),
        in_specs=specs + [per_key, per_key],
        out_specs=[
            pl.BlockSpec((step_heads, splits, height, DK), lambda i: (i, 0, 0, 0)),
            pl.BlockSpec((STEP_KEYS, rows, DK), lambda i: (i, 0, 0)),
            pl.BlockSpec((step_heads, rows, DV + DK), lambda i: (i, 0, 0)),
        ],
        out_shape=[
            pltpu.HBM((VALUE_HEAD_SET, splits, height, DK), bf16),
            pltpu.HBM((HK, rows, DK), f32),
            pltpu.HBM((VALUE_HEAD_SET, rows, DV + DK), f32),
        ],
        compiler_params=pltpu.CompilerParams(
            dimension_semantics=("arbitrary",), vmem_limit_bytes=24 << 20
        ),
        name="local_terms",
    )(
        *hbm(mixed_qkv, mixed_qkv),
        halo,
        halo,
        *hbm(conv_weight, conv_weight, beta, log_decay),
    )


def reader_kernel(
    q_ref,
    qh_ref,
    qw_ref,
    hat_ref,
    decay_ref,
    fresh_ref,
    gate_ref,
    gain_ref,
    own_ref,
    reader_ref,
    scale_ref,
):
    rows = q_ref.shape[0]
    queries = conv_silu(q_ref, qh_ref, qw_ref)
    row_ids, col_ids = square_ids(rows)
    masks = row_ids == col_ids, row_ids >= col_ids, row_ids <= col_ids
    for key in range(READER_KEYS):
        query = key_rows_hat(queries[:, key * DK : (key + 1) * DK]) * DK ** (-0.5)
        raw = three_pass_nt(halves(query), halves(hat_ref[key]))
        for member in range(GROUP):
            head = key * GROUP + member
            cum_col, fading = decay_terms(decay_ref[key, member : member + 1, :], masks)
            mixed = three_pass(fading * raw, fresh_ref[head])
            own_ref[head] = mixed[:, :DV]
            reader_ref[head] = jnp.exp(cum_col) * query - mixed[:, DV:]
            gate = gate_ref[:, head * DV : (head + 1) * DV].astype(f32)
            scale_ref[head] = silu(gate) * gain_ref[...]


def reader_terms(mixed_qkv, halo, conv_weight, log_decay, hats, fresh, out_gate, gain):
    rows = out_gate.shape[0]
    key_cols, step_heads = READER_KEYS * DK, READER_KEYS * GROUP
    value_cols = step_heads * DV
    per_head = pl.BlockSpec((step_heads, rows, DK), lambda i: (i, 0, 0))
    columns = pl.BlockSpec((rows, value_cols), lambda i: (0, i))
    return pl.pallas_call(
        reader_kernel,
        grid=(HK // READER_KEYS,),
        in_specs=[pl.BlockSpec((tall, key_cols), lambda i: (0, i)) for tall in (rows, HALO, CONV)]
        + [
            pl.BlockSpec((READER_KEYS, rows, DK), lambda i: (i, 0, 0)),
            pl.BlockSpec((READER_KEYS, GROUP, rows), lambda i: (i, 0, 0)),
            pl.BlockSpec((step_heads, rows, DV + DK), lambda i: (i, 0, 0)),
            columns,
            pl.BlockSpec((1, DV), lambda i: (0, 0)),
        ],
        out_specs=[per_head, per_head, per_head],
        out_shape=[pltpu.HBM((VALUE_HEAD_SET, rows, DK), f32)] * 3,
        compiler_params=pltpu.CompilerParams(
            dimension_semantics=("arbitrary",), vmem_limit_bytes=24 << 20
        ),
        name="reader_terms",
    )(
        *hbm(mixed_qkv),
        halo,
        *hbm(conv_weight, hats, log_decay, fresh, out_gate),
        gain[None],
    )


def scan_kernel(core_ref, near_ref, far_ref, start_ref, state_ref):
    step, core = pl.program_id(0), core_ref[0]
    block, part_rows = start_ref.shape[:2]

    @pl.when(step == 0)
    def _():
        state_ref[...] = jnp.zeros_like(state_ref)

    is_near = step % 2 == core
    added_at = pl.multiple_of(DK + core * part_rows, 16)
    state = state_ref[...]
    for place in range(block):

        def pick(span):
            return jnp.where(is_near, near_ref[place, span, :], far_ref[place, span, :])

        high, low = halves(state)
        start_ref[place] = high
        transition = pick(slice(0, DK))
        moved = dot(high, transition) + dot(low, transition)
        added = pick(pl.ds(added_at, part_rows)).astype(f32)
        terms = pick(slice(DK + 2 * part_rows, DK + 2 * part_rows + FADE_ROWS)).astype(f32)
        fade = terms[0:1] + (terms[1:2] + terms[2:3])
        state = (fade * state - moved) + added
    state_ref[...] = state


def scan_states(core, near, far, block, part_rows):
    chips, height = near.shape[:2]
    both = pl.BlockSpec((block, height, DK), lambda i, core: (i // 2, 0, 0))
    return pl.pallas_call(
        scan_kernel,
        grid_spec=pltpu.PrefetchScalarGridSpec(
            num_scalar_prefetch=1,
            grid=(2 * chips // block,),
            in_specs=[both, both],
            out_specs=pl.BlockSpec((block, part_rows, DK), lambda i, core: (i, 0, 0)),
            scratch_shapes=[pltpu.VMEM((part_rows, DK), f32)],
        ),
        out_shape=pltpu.HBM((2 * chips, part_rows, DK), bf16),
        compiler_params=pltpu.CompilerParams(
            dimension_semantics=("arbitrary",), vmem_limit_bytes=16 << 20
        ),
        name="scan_states",
    )(core, near, far)


def route_kernel(capacity, routes_ref, gates_ref, select_ref, high_ref, low_ref):
    rows = routes_ref.shape[1]
    experts = select_ref.shape[0] // capacity
    expert_ids = lax.broadcasted_iota(jnp.int32, (experts, rows), 0)
    chosen = jnp.zeros((experts, rows), jnp.bool_)
    gates = jnp.zeros((experts, rows), f32)
    for choice in range(TOPK):
        named = routes_ref[choice : choice + 1, :] == expert_ids
        chosen = chosen | named
        gates = gates + jnp.where(named, gates_ref[choice : choice + 1, :], 0.0)
    row_ids, col_ids = square_ids(rows)
    rank = dot(
        jnp.where(chosen, 1.0, 0.0).astype(bf16),
        jnp.where(row_ids < col_ids, 1.0, 0.0).astype(bf16),
    )
    slot = jnp.where(chosen, rank, -1.0).astype(jnp.int32)
    slot_ids = lax.broadcasted_iota(jnp.int32, (capacity, rows), 0)
    gathers = []
    for expert in range(experts):
        span = slice(expert * capacity, (expert + 1) * capacity)
        taken = slot_ids == slot[expert : expert + 1, :]
        select_ref[span, :] = jnp.where(taken, 1.0, 0.0).astype(bf16)
        gathers.append(jnp.where(taken, gates[expert : expert + 1, :], 0.0))
    high_ref[...], low_ref[...] = halves(jnp.concatenate(gathers, axis=0).T)


def route_tables(routes, route_gates, experts, capacity):
    rows = routes.shape[0]
    slots = experts * capacity
    return pl.pallas_call(
        functools.partial(route_kernel, capacity),
        out_shape=[
            pltpu.HBM((slots, rows), bf16),
            pltpu.HBM((rows, slots), bf16),
            pltpu.HBM((rows, slots), bf16),
        ],
        name="route_tables",
    )(routes.T, route_gates.T)


def mixer_kernel(
    state_ref,
    moe_gain_ref,
    select_hbm,
    own_hbm,
    reader_hbm,
    scale_hbm,
    resid_hbm,
    middle_hbm,
    mixer_hbm,
    rows_hbm,
    select_ref,
    middle_ref,
    own_ref,
    reader_ref,
    scale_ref,
    resid_ref,
    mixer_ref,
    rows_ref,
    in_sems,
    mixer_sems,
    rows_sems,
    middle_sems,
    select_sem,
):
    groups = in_sems.shape[0]
    heads = VALUE_HEAD_SET // groups
    loads, stores = [], []
    for group in range(groups):
        part, columns = pl.ds(group * heads, heads), pl.ds(group * heads * DV, heads * DV)
        loads.append(
            [
                pltpu.make_async_copy(source, target, in_sems.at[group, place])
                for place, (source, target) in enumerate(
                    (
                        (own_hbm.at[part], own_ref.at[part]),
                        (reader_hbm.at[part], reader_ref.at[part]),
                        (scale_hbm.at[part], scale_ref.at[part]),
                        (resid_hbm.at[:, columns], resid_ref.at[:, columns]),
                    )
                )
            ]
        )
        for load in loads[-1]:
            load.start()
    select_load = pltpu.make_async_copy(select_hbm, select_ref, select_sem)
    select_load.start()

    squares = None
    for group in range(groups):
        for load in loads[group]:
            load.wait()
        for head in range(group * heads, (group + 1) * heads):
            span = slice(head * DV, (head + 1) * DV)
            if len(state_ref.shape) == 3:
                state = state_ref[head]
            else:
                block = state_ref.shape[2]
                pieces = [state_ref[head // block, core, head % block] for core in range(2)]
                state = jnp.concatenate(pieces, axis=0)
            high, low = halves(reader_ref[head])
            head_out = own_ref[head] + (dot_nt(high, state) + dot_nt(low, state))
            spread = lax.rsqrt(jnp.mean(head_out * head_out, axis=1, keepdims=True) + 1e-06)
            mixed = (head_out * spread * scale_ref[head]).astype(bf16)
            mixer_ref[:, span] = mixed
            middle = resid_ref[:, span].astype(f32) + mixed.astype(f32)
            middle_ref[head] = middle
            part = jnp.sum(middle * middle, axis=1, keepdims=True)
            squares = part if squares is None else squares + part
        columns = pl.ds(group * heads * DV, heads * DV)
        part = pl.ds(group * heads, heads)
        stores.append(
            pltpu.make_async_copy(middle_ref.at[part], middle_hbm.at[part], middle_sems.at[group])
        )
        stores[-1].start()
        stores.append(
            pltpu.make_async_copy(
                mixer_ref.at[:, columns], mixer_hbm.at[:, columns], mixer_sems.at[group]
            )
        )
        stores[-1].start()

    spread = lax.rsqrt(squares / resid_ref.shape[1] + 1e-06)
    select_load.wait()
    select = select_ref[...]
    for group in range(groups):
        for head in range(group * heads, (group + 1) * heads):
            span = slice(head * DV, (head + 1) * DV)
            moe_input = (middle_ref[head] * spread * moe_gain_ref[:, span]).astype(bf16)
            rows_ref[:, span] = dot(select, moe_input).astype(bf16)
        columns = pl.ds(group * heads * DV, heads * DV)
        stores.append(
            pltpu.make_async_copy(
                rows_ref.at[:, columns], rows_hbm.at[:, columns], rows_sems.at[group]
            )
        )
        stores[-1].start()
    for store in stores:
        store.wait()


def mixer(own, reader, scale, resid, select, state, moe_gain):
    rows, width = resid.shape
    slots, groups = select.shape[0], 4
    local, remote = pl.BlockSpec(memory_space=pltpu.VMEM), pl.BlockSpec(memory_space=pltpu.HBM)
    return pl.pallas_call(
        mixer_kernel,
        in_specs=[local] * 2 + [remote] * 5,
        out_specs=[remote] * 3,
        out_shape=[
            pltpu.HBM((VALUE_HEAD_SET, rows, DV), f32),
            pltpu.HBM((rows, width), bf16),
            pltpu.HBM((slots, width), bf16),
        ],
        scratch_shapes=[pltpu.VMEM((slots, rows), bf16)]
        + [pltpu.VMEM((VALUE_HEAD_SET, rows, DV), f32)] * 4
        + [
            pltpu.VMEM((rows, width), bf16),
            pltpu.VMEM((rows, width), bf16),
            pltpu.VMEM((slots, width), bf16),
            pltpu.SemaphoreType.DMA((groups, 4)),
            pltpu.SemaphoreType.DMA((groups,)),
            pltpu.SemaphoreType.DMA((groups,)),
            pltpu.SemaphoreType.DMA((groups,)),
            pltpu.SemaphoreType.DMA,
        ],
        compiler_params=pltpu.CompilerParams(vmem_limit_bytes=24 << 20),
        name="mixer",
    )(state, moe_gain[None], *hbm(select, own, reader, scale, resid))


def start_loads(sources, buffer_ref, sems):
    loads = [
        pltpu.make_async_copy(source, buffer_ref.at[place], sems.at[place])
        for place, source in enumerate(sources)
    ]
    for load in loads:
        load.start()
    return loads


def expert_in_kernel(order_ref, rows_ref, *refs):
    sources, (result_ref, buffer_ref, sems) = refs[:-3], refs[-3:]
    depth, projected = buffer_ref.shape[1], None
    for place, load in enumerate(start_loads(sources, buffer_ref, sems)):
        start = pl.multiple_of(order_ref[place] * depth, depth)
        load.wait()
        term = dot(rows_ref[:, pl.ds(start, depth)], buffer_ref[place])
        projected = term if projected is None else projected + term
    result_ref[...] = (silu(projected[:, :MOE_H]) * projected[:, MOE_H:]).astype(bf16)


def expert_out_kernel(order_ref, activated_ref, *refs):
    sources, (result_ref, buffer_ref, sems) = refs[:-3], refs[-3:]
    cols, activated = buffer_ref.shape[2], activated_ref[...]
    for place, load in enumerate(start_loads(sources, buffer_ref, sems)):
        start = pl.multiple_of(order_ref[place] * cols, cols)
        load.wait()
        result_ref[:, pl.ds(start, cols)] = dot(activated, buffer_ref[place]).astype(bf16)


def expert_call(kernel, name, order, rows, parts, width):
    local, remote = pl.BlockSpec(memory_space=pltpu.VMEM), pl.BlockSpec(memory_space=pltpu.HBM)
    return pl.pallas_call(
        kernel,
        in_specs=[pl.BlockSpec(memory_space=pltpu.SMEM), local] + [remote] * len(parts),
        out_specs=local,
        out_shape=jax.ShapeDtypeStruct((rows.shape[0], width), bf16),
        scratch_shapes=[
            pltpu.VMEM((len(parts),) + parts[0].shape, bf16),
            pltpu.SemaphoreType.DMA((len(parts),)),
        ],
        compiler_params=pltpu.CompilerParams(vmem_limit_bytes=24 << 20),
        name=name,
    )(order, rows, *hbm(*parts))


def expert_in(order, rows, parts):
    rows = rows.reshape(-1, rows.shape[-1])
    return expert_call(expert_in_kernel, "expert_in", order, rows, parts, MOE_H)


def expert_out(order, activated, parts, width):
    return expert_call(expert_out_kernel, "expert_out", order, activated, parts, width)


def combine_kernel(high_ref, low_ref, middle_ref, rows_ref, out_hbm, out_ref, sems):
    high, low = high_ref[...], low_ref[...]
    groups = sems.shape[0]
    heads, stores = middle_ref.shape[0] // groups, []
    for group in range(groups):
        for head in range(group * heads, (group + 1) * heads):
            span = slice(head * DV, (head + 1) * DV)
            rows = rows_ref[:, span]
            summed = dot(high, rows) + dot(low, rows)
            out_ref[:, span] = (middle_ref[head] + summed).astype(bf16)
        columns = pl.ds(group * heads * DV, heads * DV)
        stores.append(
            pltpu.make_async_copy(out_ref.at[:, columns], out_hbm.at[:, columns], sems.at[group])
        )
        stores[-1].start()
    for store in stores:
        store.wait()


def combine(high, low, middle, rows):
    count, width = middle.shape[1], rows.shape[1]
    groups = 4
    return pl.pallas_call(
        combine_kernel,
        in_specs=[pl.BlockSpec(memory_space=pltpu.VMEM)] * 4,
        out_specs=pl.BlockSpec(memory_space=pltpu.HBM),
        out_shape=pltpu.HBM((count, width), bf16),
        scratch_shapes=[
            pltpu.VMEM((count, width), bf16),
            pltpu.SemaphoreType.DMA((groups,)),
        ],
        compiler_params=pltpu.CompilerParams(vmem_limit_bytes=24 << 20),
        name="combine",
    )(high, low, middle, rows)


def after(value, earlier):
    return lax.optimization_barrier((value, earlier))[0]


def across_halves(value, flip):
    pairs = [
        (core * 2 + half, half * 2 + (core ^ flip)) for core in range(2) for half in range(2)
    ]
    return lax.ppermute(value, ("core", "half"), pairs)


def along_y(value, y_count):
    moved = [value]
    for shift in range(1, y_count):
        pairs = [(source, (source + shift) % y_count) for source in range(y_count)]
        moved.append(lax.ppermute(value, "y", pairs))
    return moved


def shards(
    resid,
    mixed_qkv,
    out_gate,
    beta,
    log_decay,
    conv_weight,
    head_gain,
    moe_gain,
    routes,
    route_gates,
    w_in,
    w_out,
):
    every = ("y", "core", "half", "rest")
    y_count, rest_count = lax.axis_size("y"), lax.axis_size("rest")
    count = lax.axis_size(every)
    experts = 2 * rest_count
    chips, block = count // 2, 2 * rest_count
    splits = chips // VALUE_HEAD_SET
    part = DV // (2 * splits)
    part_rows = round_up(part, 16)
    capacity = round_up(
        max(2, (5 * TOK_DEV * TOPK + 4 * experts - 1) // (4 * experts)), 16
    )
    rows = mixed_qkv.shape[0]
    beta, log_decay = (value.reshape(HK, GROUP, rows) for value in (beta, log_decay))
    tie = lax.optimization_barrier

    rim = mixed_qkv[rows - HALO :]
    halo = lax.ppermute(rim, every, [(source, source + 1) for source in range(count - 1)])
    in_first = across_halves(after(w_in[0], rim), 0)
    send, hats, fresh = local_terms(
        mixed_qkv, halo, conv_weight, beta, log_decay, splits, part, part_rows
    )

    near = lax.all_to_all(
        send.reshape(chips, -1, DK),
        ("y", "half", "rest"),
        split_axis=0,
        concat_axis=0,
        tiled=True,
    )
    hats, in_first = tie((hats, in_first))
    own, reader, scale = reader_terms(
        mixed_qkv, halo, conv_weight, log_decay, hats, fresh, out_gate, head_gain
    )
    select, *gather = route_tables(routes, route_gates, experts, capacity)
    in_first = along_y(in_first, y_count)
    out_first = across_halves(after(w_out[0], send), 0)
    near, in_first, out_first, own, select = tie((near, in_first, out_first, own, select))

    in_second = across_halves(after(w_in[0], near), 1)
    far = lax.ppermute(near, "core", [(0, 1), (1, 0)])
    core = lax.axis_index("core").astype(jnp.int32).reshape(1)
    starts = scan_states(core, near, far, block, part_rows)
    states = lax.all_to_all(starts, every, split_axis=0, concat_axis=0, tiled=True)
    out_first = along_y(out_first, y_count)
    states, in_second, out_first = tie((states, in_second, out_first))

    states = states.reshape(y_count, 2, block, part_rows, DK)
    if part < part_rows or splits > 1:
        states = states[:, :, :, :part].transpose(0, 2, 1, 3, 4)
        states = states.reshape(VALUE_HEAD_SET, DV, DK)
    middle, mixer_out, send_rows = mixer(
        own, reader, scale, resid, select, states, moe_gain
    )
    in_second = along_y(after(in_second, send_rows), y_count)
    out_second = across_halves(after(w_out[0], send_rows), 1)
    out_second = along_y(out_second, y_count)
    exchange = functools.partial(
        lax.all_to_all, axis_name=("core", "rest"), split_axis=0, concat_axis=0, tiled=True
    )
    y_index, half = lax.axis_index("y"), lax.axis_index("half")
    order = jnp.stack(
        [
            (y_index - shift) % y_count * 2 + (half ^ flip)
            for flip in range(2)
            for shift in range(y_count)
        ]
    )
    activated = expert_in(order, exchange(send_rows), in_first + in_second)
    expert_rows = expert_out(order, activated, out_first + out_second, send_rows.shape[1])
    return mixer_out, combine(*gather, middle, exchange(expert_rows))


def solution(mesh):
    ctx_count, ep_count = mesh.shape["ctx"], mesh.shape["ep"]
    names = ("y", "core", "half", "rest")
    fine = Mesh(mesh.devices.reshape(ctx_count // 2, 2, 2, ep_count // 2), names)
    split_rows, split_cols = P(names, None), P(None, names)
    ctx, ep = names[:2], names[2:]
    return jax.shard_map(
        shards,
        mesh=fine,
        in_specs=(
            split_rows,
            split_rows,
            split_rows,
            split_cols,
            split_cols,
            P(),
            P(),
            P(),
            split_rows,
            split_rows,
            P(ep, ctx, None),
            P(ep, None, ctx),
        ),
        out_specs=(split_rows, split_rows),
        check_vma=False,
    )
```
